768 devices in a mesh: comp: 16 (over y_hi, x, core), dom: 48 (over y_lo, z).
Axes of the slice: x: 4, y: 8 (y_hi: 2, y_lo: 4; y = y_hi * 4 + y_lo), z: 12, core: 2. Of those that a mesh axis runs over, the one named last changes fastest.
Arguments:
- action: float32 [1152, 98304], P('comp', 'dom'), may hold values from 0.1 to 1
- coef_one: float32 [1152], P('comp'), may hold values from 0.1 to 0.6
- coef_two: float32 [1152], P('comp'), may hold values from 0.1 to 0.6
- transport_one: bfloat16 [768, 3, 128, 128], P('dom'), may hold values from -0.3125 to 0.3125
- transport_two: bfloat16 [768, 3, 128, 128], P('dom'), may hold values from -0.3125 to 0.3125
- block_cols: int32 [768, 3], P('dom'), may hold values from 0 to 17, as said below
- quad_one: bfloat16 [1152, 1152], replicated, may hold values from -0.1875 to 0.1875
- quad_two: bfloat16 [1152, 1152], replicated, may hold values from -0.1875 to 0.1875
Outputs:
- updated: float32 [48, 2048, 1152], P('dom', 'comp')
The draws below stay inside these ranges and needn't reach their ends.
Inputs may be any that keep to these rules, and one draw needn't show every extreme that they name: `block_cols`: entry 1 of every block row is the block just before it and entry 2 the block just after it, in the extended counting; entry 0 is any block of the extended range.
All inputs are finite; a program needn't handle non-finite values.
Results may differ from the reference program's by a relative error of at most 0.0067.
Values may be sent and summed in bfloat16 or wider, within the bound.
No kernel may reach another device: no remote copies, remote signals or barrier semaphores. Data moves between devices by JAX's collectives and lax.ppermute only.
A program may use at most 32 MiB of HBM per device.

```python
import math
import jax
import jax.numpy as jnp
from jax import lax

K = 1152
BLOCK = 128
NNZ = 3
SUBSTEPS = 4
NBLK_DEV = 16
CELLS_DEV = 2048
DOMAINS = 48
BLOCKS = 768
CELLS = 98304


def draw_block_cols(key, part):
    local = (jnp.arange(BLOCKS, dtype=jnp.int32) % NBLK_DEV).astype(jnp.int32)
    chosen = jax.random.randint(jax.random.fold_in(key, 11), (BLOCKS,), 0, NBLK_DEV + 2, dtype=jnp.int32)
    return jnp.stack([chosen, local, local + 2], axis=1).astype(jnp.int32)


def block_levels(own_key, extent, cuts, low, largest):
    def one(position, parts):
        steps = jax.random.uniform(jax.random.fold_in(jax.random.fold_in(own_key, 6), position), (parts,), jnp.float32, low / len(cuts), largest / len(cuts))
        return jnp.repeat(jnp.exp(steps), extent[position] // parts).reshape((-1,) + (1,) * (len(extent) - position - 1))

    gain = one(*cuts[0])
    for cut in cuts[1:]:
        gain = gain * one(*cut)
    return gain


def scatter_about(rng, dims, deviation, limit, pieces=(), kind=jnp.bfloat16):
    values = jax.random.normal(rng, dims, jnp.float32) * deviation
    if len(pieces) > 0:
        values = block_levels(rng, dims, pieces, -0.22, 0.18) * values
    return jnp.clip(values, min=-limit, max=limit).astype(kind)


def setup_inputs(seed: int = 0) -> dict:
    streams_of = jax.random.split(jax.random.key(seed), 9)
    action = jnp.clip(jnp.exp(math.log(1.0) - 2.3025851 * jax.random.uniform(streams_of[0], (K, CELLS), jnp.float32) ** block_levels(streams_of[0], (K, CELLS), ((0, 16), (1, 48)), -0.2, 0.2)), 0.1, 1.0)
    coef_one = jnp.clip(jnp.exp(math.log(0.6) - 1.7917595 * jax.random.uniform(streams_of[1], (K,), jnp.float32) ** block_levels(streams_of[1], (K,), ((0, 16),), -0.2, 0.2)), 0.1, 0.6)
    coef_two = jnp.clip(jnp.exp(math.log(0.6) - 1.7917595 * jax.random.uniform(streams_of[2], (K,), jnp.float32) ** block_levels(streams_of[2], (K,), ((0, 16),), -0.2, 0.2)), 0.1, 0.6)
    transport_one = scatter_about(streams_of[3], (BLOCKS, NNZ, BLOCK, BLOCK), (NNZ * BLOCK) ** -0.5, 0.3125, ((0, 48),))
    transport_two = scatter_about(streams_of[4], (BLOCKS, NNZ, BLOCK, BLOCK), (NNZ * BLOCK) ** -0.5, 0.3125, ((0, 48),))
    block_cols = draw_block_cols(jax.random.fold_in(streams_of[8], 71), 0)
    quad_one = scatter_about(streams_of[6], (K, K), K ** -0.5, 0.1875)
    quad_two = scatter_about(streams_of[7], (K, K), K ** -0.5, 0.1875)
    return {"action": action, "coef_one": coef_one, "coef_two": coef_two, "transport_one": transport_one, "transport_two": transport_two, "block_cols": block_cols, "quad_one": quad_one, "quad_two": quad_two}


keep_share = 0.25


def reference(action, coef_one, coef_two, transport_one, transport_two, block_cols, quad_one, quad_two):
    nblocks = block_cols.shape[0]
    owner = (jnp.arange(nblocks, dtype=jnp.int32) // NBLK_DEV) * NBLK_DEV
    located = (owner[:, None] + block_cols).astype(jnp.int32)
    one_wide = transport_one.astype(jnp.float32)
    two_wide = transport_two.astype(jnp.float32)
    field = action
    for substep in range(SUBSTEPS):
        rounded = lax.optimization_barrier(field.astype(jnp.bfloat16))
        padded = jnp.pad(rounded, ((0, 0), (BLOCK, BLOCK))).reshape(K, nblocks + 2, BLOCK)
        gathered = padded[:, located].astype(jnp.float32)
        flow_one = jnp.einsum('kbjc,bjcd->kbd', gathered, one_wide).reshape(K, CELLS)
        flow_two = jnp.einsum('kbjc,bjcd->kbd', gathered, two_wide).reshape(K, CELLS)
        moved = field + coef_one[:, None] * flow_one + coef_two[:, None] * flow_two
        field = jnp.maximum(moved, keep_share * field)
    final = lax.optimization_barrier(field.astype(jnp.bfloat16))
    cells = final.T
    first = jnp.dot(cells, quad_one, preferred_element_type=jnp.float32)
    second = jnp.dot(cells, quad_two, preferred_element_type=jnp.float32)
    cell_wide = cells.astype(jnp.float32)
    result = cell_wide + 0.5 * (first * cell_wide - second * cell_wide * cell_wide)
    return result.reshape(DOMAINS, CELLS_DEV, K)
```

```python
import functools

import jax
import jax.numpy as jnp
from jax import lax
from jax.experimental import pallas as pl
from jax.experimental.pallas import tpu as pltpu
from jax.sharding import PartitionSpec as P

SUBSTEPS = 4
KEEP = 0.25


def in_vmem(x):
    return pltpu.with_memory_space_constraint(x, pltpu.VMEM)


def whole():
    return pl.BlockSpec(memory_space=pltpu.VMEM)


def call(body, outs, n_vmem, limit, name):
    return pl.pallas_call(
        body,
        out_shape=[pltpu.VMEM(s, d) for s, d in outs],
        grid_spec=pltpu.PrefetchScalarGridSpec(
            num_scalar_prefetch=1,
            grid=(),
            in_specs=[whole()] * n_vmem,
            out_specs=[whole()] * len(outs),
        ),
        compiler_params=pltpu.CompilerParams(vmem_limit_bytes=limit),
        name=name,
    )


def row_update(b, chosen, before, after, value, one, two, coef_one, coef_two):
    width = value.shape[1]
    gathered = jnp.concatenate([chosen, before, after], axis=1)
    both = jnp.concatenate([one, two], axis=1)
    flow = jnp.dot(gathered, both, preferred_element_type=jnp.float32)
    moved = value + coef_one * flow[:, :width] + coef_two * flow[:, width:]
    return jnp.maximum(moved, KEEP * value)


def chosen_block(e, left, right, blocks_ref):
    n = blocks_ref.shape[0]
    inner = blocks_ref[jnp.clip(e - 1, 0, n - 1)]
    return jnp.where(e == 0, left, jnp.where(e == n + 1, right, inner))


def edge_kernel(cols, left_ref, right_ref, blocks_ref, first_ref, last_ref, one_ref, two_ref, c1_ref, c2_ref, *outs):
    first16, last16, first32, last32 = outs
    n, rows, width = blocks_ref.shape
    left, right = left_ref[...], right_ref[...]
    c1, c2 = c1_ref[...], c2_ref[...]
    for b, value_ref, out16, out32 in ((0, first_ref, first16, first32), (n - 1, last_ref, last16, last32)):
        new = row_update(
            b,
            chosen_block(cols[3 * b], left, right, blocks_ref),
            left if b == 0 else blocks_ref[b - 1],
            right if b == n - 1 else blocks_ref[b + 1],
            value_ref[...],
            one_ref[b].reshape(-1, width),
            two_ref[b].reshape(-1, width),
            c1,
            c2,
        )
        out32[...] = new
        out16[...] = new.astype(jnp.bfloat16)


def inner_kernel(cols, left_ref, right_ref, blocks_ref, field_ref, first16, last16, one_ref, two_ref, c1_ref, c2_ref, *outs):
    out16, out32 = outs
    n, rows, width = blocks_ref.shape
    left, right = left_ref[...], right_ref[...]
    c1, c2 = c1_ref[...], c2_ref[...]
    out16[0] = first16[...]
    out16[n - 1] = last16[...]
    for b in range(1, n - 1):
        new = row_update(
            b,
            chosen_block(cols[3 * b], left, right, blocks_ref),
            blocks_ref[b - 1],
            blocks_ref[b + 1],
            field_ref[b],
            one_ref[b].reshape(-1, width),
            two_ref[b].reshape(-1, width),
            c1,
            c2,
        )
        out32[b] = new
        out16[b] = new.astype(jnp.bfloat16)


def last_kernel(cols, left_ref, right_ref, blocks_ref, field_ref, first_ref, last_ref, one_ref, two_ref, c1_ref, c2_ref, *outs):
    (out16,) = outs
    n, rows, width = blocks_ref.shape
    left, right = left_ref[...], right_ref[...]
    c1, c2 = c1_ref[...], c2_ref[...]
    for b in range(n):
        value = first_ref[...] if b == 0 else last_ref[...] if b == n - 1 else field_ref[b]
        new = row_update(
            b,
            chosen_block(cols[3 * b], left, right, blocks_ref),
            left if b == 0 else blocks_ref[b - 1],
            right if b == n - 1 else blocks_ref[b + 1],
            value,
            one_ref[b].reshape(-1, width),
            two_ref[b].reshape(-1, width),
            c1,
            c2,
        )
        out16[b] = new.astype(jnp.bfloat16)


def load_kernel(cols, action_ref, out16, out32, first32, last32):
    n, rows, width = out16.shape
    for b in range(n):
        value = action_ref[:, b * width : (b + 1) * width]
        out32[b] = value
        out16[b] = value.astype(jnp.bfloat16)
    first32[...] = action_ref[:, :width]
    last32[...] = action_ref[:, (n - 1) * width :]


def source_kernel(cells_ref, one_ref, two_ref, out_ref):
    step = pl.program_id(0)
    tile = out_ref.shape[2]
    cells = cells_ref[...].T
    own = cells_ref[pl.ds(pl.multiple_of(step * tile, tile), tile), :].astype(jnp.float32).T
    first = jnp.dot(cells, one_ref[...], preferred_element_type=jnp.float32)
    second = jnp.dot(cells, two_ref[...], preferred_element_type=jnp.float32)
    out_ref[0] = own + 0.5 * (first * own - second * own * own)


def source_terms(exchanged, quad_one, quad_two):
    comps, cells = exchanged.shape
    tile = 384
    return pl.pallas_call(
        source_kernel,
        out_shape=jax.ShapeDtypeStruct((1, cells, comps), jnp.float32),
        grid=(comps // tile,),
        in_specs=[
            pl.BlockSpec((comps, cells), lambda i: (0, 0)),
            pl.BlockSpec((comps, tile), lambda i: (0, i)),
            pl.BlockSpec((comps, tile), lambda i: (0, i)),
        ],
        out_specs=pl.BlockSpec((1, cells, tile), lambda i: (0, 0, i)),
        compiler_params=pltpu.CompilerParams(vmem_limit_bytes=16 << 20),
        name="source_terms",
    )(exchanged, quad_one, quad_two)


def per_device(
    action, coef_one, coef_two, transport_one, transport_two, block_cols, quad_one, quad_two
):
    rows, cells_dev = action.shape
    n, _, width, _ = transport_one.shape
    dom = lax.axis_size("dom")
    up = [(i, i + 1) for i in range(dom - 1)]
    down = [(i + 1, i) for i in range(dom - 1)]
    bf16, f32 = jnp.bfloat16, jnp.float32
    block, blocks = (rows, width), (n, rows, width)

    cols = block_cols.reshape(-1)
    one, two = in_vmem(transport_one), in_vmem(transport_two)
    c1 = in_vmem(jnp.broadcast_to(coef_one[:, None], block))
    c2 = in_vmem(jnp.broadcast_to(coef_two[:, None], block))

    first = action[:, :width].astype(bf16)
    last = action[:, cells_dev - width :].astype(bf16)
    left = lax.ppermute(last, "dom", up)
    right = lax.ppermute(first, "dom", down)
    value16, value32, first32, last32 = call(
        load_kernel, [(blocks, bf16), (blocks, f32), (block, f32), (block, f32)], 1, 4 << 20, "load"
    )(cols, in_vmem(action))
    for substep in range(SUBSTEPS - 1):
        first, last, first32, last32 = call(
            edge_kernel, [(block, bf16), (block, bf16), (block, f32), (block, f32)], 9, 4 << 20, "edges"
        )(cols, in_vmem(left), in_vmem(right), value16, first32, last32, one, two, c1, c2)
        new_left = lax.ppermute(last, "dom", up)
        new_right = lax.ppermute(first, "dom", down)
        value16, value32 = call(
            inner_kernel, [(blocks, bf16), (blocks, f32)], 10, 4 << 20, "inner"
        )(cols, in_vmem(left), in_vmem(right), value16, value32, first, last, one, two, c1, c2)
        left, right = new_left, new_right
    (final,) = call(last_kernel, [(blocks, bf16)], 10, 4 << 20, "last")(
        cols, in_vmem(left), in_vmem(right), value16, value32, first32, last32, one, two, c1, c2
    )
    exchanged = lax.all_to_all(final, "comp", split_axis=0, concat_axis=0, tiled=True)
    return source_terms(exchanged.reshape(n * rows, width), quad_one, quad_two)


def solution(mesh):
    in_specs = (
        P("comp", "dom"),
        P("comp"),
        P("comp"),
        P("dom", None, None, None),
        P("dom", None, None, None),
        P("dom", None),
        P(),
        P(),
    )
    out_specs = P("dom", "comp", None)
    return jax.shard_map(
        per_device, mesh=mesh, in_specs=in_specs, out_specs=out_specs, check_vma=False
    )
```

```python
import jax
import jax.numpy as jnp
from jax import lax
from jax.experimental import pallas as pl
from jax.experimental.pallas import tpu as pltpu
from jax.sharding import PartitionSpec as P

SUBSTEPS = 4
KEEP = 0.25


def in_vmem(x):
    return pltpu.with_memory_space_constraint(x, pltpu.VMEM)


def in_hbm(x):
    return pltpu.with_memory_space_constraint(x, pltpu.HBM)


def in_smem(x):
    return pltpu.with_memory_space_constraint(x, pltpu.SMEM)


def vmem():
    return pl.BlockSpec(memory_space=pltpu.VMEM)


def smem():
    return pl.BlockSpec(memory_space=pltpu.SMEM)


def hbm():
    return pl.BlockSpec(memory_space=pltpu.HBM)


def call(body, outs, in_specs, name, scratch=(), limit=4 << 20):
    return pl.pallas_call(
        body,
        out_shape=[pltpu.VMEM(s, d) for s, d in outs],
        in_specs=in_specs,
        out_specs=[vmem()] * len(outs),
        scratch_shapes=list(scratch),
        compiler_params=pltpu.CompilerParams(vmem_limit_bytes=limit),
        name=name,
    )


def row_update(b, chosen, before, after, value, one, two, coef_one, coef_two):
    width = value.shape[1]
    gathered = jnp.concatenate([chosen, before, after], axis=1)
    both = jnp.concatenate([one, two], axis=1)
    flow = jnp.dot(gathered, both, preferred_element_type=jnp.float32)
    moved = value + coef_one * flow[:, :width] + coef_two * flow[:, width:]
    return jnp.maximum(moved, KEEP * value)


def chosen_block(e, left, right, blocks_ref):
    n = blocks_ref.shape[0]
    inner = blocks_ref[jnp.clip(e - 1, 0, n - 1)]
    return jnp.where(e == 0, left, jnp.where(e == n + 1, right, inner))


def edge_kernel(cols, left_ref, right_ref, blocks_ref, first_ref, last_ref, one_ref, two_ref, c1_ref, c2_ref, *outs):
    last16, first16, last32, first32 = outs
    n, rows, width = blocks_ref.shape
    left, right = left_ref[...], right_ref[...]
    c1, c2 = c1_ref[...], c2_ref[...]
    for b, value_ref, out16, out32 in ((0, first_ref, first16, first32), (n - 1, last_ref, last16, last32)):
        new = row_update(
            b,
            chosen_block(cols[0, b], left, right, blocks_ref),
            left if b == 0 else blocks_ref[b - 1],
            right if b == n - 1 else blocks_ref[b + 1],
            value_ref[...],
            one_ref[b].reshape(-1, width),
            two_ref[b].reshape(-1, width),
            c1,
            c2,
        )
        out32[...] = new
        out16[...] = new.astype(jnp.bfloat16)


def inner_kernel(cols, left_ref, right_ref, blocks_ref, field_ref, first16, last16, one_ref, two_ref, c1_ref, c2_ref, *outs):
    out16, out32 = outs
    n, rows, width = blocks_ref.shape
    left, right = left_ref[...], right_ref[...]
    c1, c2 = c1_ref[...], c2_ref[...]
    out16[0] = first16[...]
    out16[n - 1] = last16[...]
    for b in range(1, n - 1):
        new = row_update(
            b,
            chosen_block(cols[0, b], left, right, blocks_ref),
            blocks_ref[b - 1],
            blocks_ref[b + 1],
            field_ref[b],
            one_ref[b].reshape(-1, width),
            two_ref[b].reshape(-1, width),
            c1,
            c2,
        )
        out32[b] = new
        out16[b] = new.astype(jnp.bfloat16)


def last_kernel(cols, left_ref, right_ref, blocks_ref, field_ref, first_ref, last_ref, one_ref, two_ref, c1_ref, c2_ref, *outs):
    (out16,) = outs
    n, rows, width = blocks_ref.shape
    left, right = left_ref[...], right_ref[...]
    c1, c2 = c1_ref[...], c2_ref[...]
    for b in range(n):
        value = first_ref[...] if b == 0 else last_ref[...] if b == n - 1 else field_ref[b]
        new = row_update(
            b,
            chosen_block(cols[0, b], left, right, blocks_ref),
            left if b == 0 else blocks_ref[b - 1],
            right if b == n - 1 else blocks_ref[b + 1],
            value,
            one_ref[b].reshape(-1, width),
            two_ref[b].reshape(-1, width),
            c1,
            c2,
        )
        out16[b] = new.astype(jnp.bfloat16)


def begin_kernel(action_ref, last16, first16, buffers, sems):
    width = first16.shape[1]
    cells = action_ref.shape[1]
    copies = [
        pltpu.make_async_copy(action_ref.at[:, pl.ds(cells - width, width)], buffers.at[0], sems.at[0]),
        pltpu.make_async_copy(action_ref.at[:, pl.ds(0, width)], buffers.at[1], sems.at[1]),
    ]
    for copy in copies:
        copy.start()
    for copy, out, i in zip(copies, (last16, first16), (0, 1)):
        copy.wait()
        out[...] = buffers[i].astype(jnp.bfloat16)


def load_kernel(action_ref, coef_one_ref, coef_two_ref, one_hbm, two_hbm, *refs):
    out16, out32, first32, last32, one, two, c1, c2, sems = refs
    n, rows, width = out16.shape
    copies = [
        pltpu.make_async_copy(action_ref.at[:, pl.ds(b * width, width)], out32.at[b], sems.at[b])
        for b in range(n)
    ]
    weights = [
        pltpu.make_async_copy(one_hbm, one, sems.at[n]),
        pltpu.make_async_copy(two_hbm, two, sems.at[n + 1]),
    ]
    for copy in copies + weights:
        copy.start()
    c1[...] = jnp.broadcast_to(coef_one_ref[...], (width, rows)).T
    c2[...] = jnp.broadcast_to(coef_two_ref[...], (width, rows)).T
    for b in range(n):
        copies[b].wait()
        out16[b] = out32[b].astype(jnp.bfloat16)
    first32[...] = out32[0]
    last32[...] = out32[n - 1]
    for copy in weights:
        copy.wait()


def source_kernel(cells_ref, one_ref, two_ref, out_hbm, buffers, sems):
    steps, _, tile = buffers.shape
    cells = cells_ref[...].T
    copies = []
    for i in range(steps):
        at = slice(i * tile, (i + 1) * tile)
        own = cells[:, at].astype(jnp.float32)
        first = jnp.dot(cells, one_ref[:, at], preferred_element_type=jnp.float32)
        second = jnp.dot(cells, two_ref[:, at], preferred_element_type=jnp.float32)
        buffers[i] = own + 0.5 * (first * own - second * own * own)
        copies.append(pltpu.make_async_copy(buffers.at[i], out_hbm.at[0, :, pl.ds(i * tile, tile)], sems.at[i]))
        copies[-1].start()
    for copy in copies:
        copy.wait()


def source_terms(exchanged, quad_one, quad_two):
    comps, cells = exchanged.shape
    tile = 384
    steps = comps // tile
    return pl.pallas_call(
        source_kernel,
        out_shape=jax.ShapeDtypeStruct((1, cells, comps), jnp.float32),
        in_specs=[vmem()] * 3,
        out_specs=hbm(),
        scratch_shapes=[
            pltpu.VMEM((steps, cells, tile), jnp.float32),
            pltpu.SemaphoreType.DMA((steps,)),
        ],
        compiler_params=pltpu.CompilerParams(vmem_limit_bytes=8 << 20),
        name="source_terms",
    )(in_vmem(exchanged), in_vmem(quad_one), in_vmem(quad_two))


def per_device(
    action, coef_one, coef_two, transport_one, transport_two, block_cols, quad_one, quad_two
):
    rows, cells_dev = action.shape
    n, nnz, width, _ = transport_one.shape
    dom = lax.axis_size("dom")
    up = [(i, i + 1) for i in range(dom - 1)]
    down = [(i + 1, i) for i in range(dom - 1)]
    bf16, f32 = jnp.bfloat16, jnp.float32
    block, blocks, weights = (rows, width), (n, rows, width), (n, nnz, width, width)

    cols = in_smem(block_cols.T)
    last, first = call(
        begin_kernel,
        [(block, bf16), (block, bf16)],
        [hbm()],
        "begin",
        [pltpu.VMEM((2, rows, width), f32), pltpu.SemaphoreType.DMA((2,))],
    )(in_hbm(action))
    left = lax.ppermute(last, "dom", up)
    right = lax.ppermute(first, "dom", down)
    value16, value32, first32, last32, one, two, c1, c2 = call(
        load_kernel,
        [(blocks, bf16), (blocks, f32), (block, f32), (block, f32), (weights, bf16), (weights, bf16), (block, f32), (block, f32)],
        [hbm(), vmem(), vmem(), hbm(), hbm()],
        "load",
        [pltpu.SemaphoreType.DMA((n + 2,))],
    )(
        in_hbm(action), coef_one.reshape(1, rows), coef_two.reshape(1, rows), in_hbm(transport_one), in_hbm(transport_two)
    )
    for substep in range(SUBSTEPS - 1):
        last, first, last32, first32 = call(
            edge_kernel, [(block, bf16), (block, bf16), (block, f32), (block, f32)], [smem()] + [vmem()] * 9, "edges"
        )(cols, in_vmem(left), in_vmem(right), value16, first32, last32, one, two, c1, c2)
        new_left = lax.ppermute(last, "dom", up)
        new_right = lax.ppermute(first, "dom", down)
        value16, value32 = call(
            inner_kernel, [(blocks, bf16), (blocks, f32)], [smem()] + [vmem()] * 10, "inner"
        )(cols, in_vmem(left), in_vmem(right), value16, value32, first, last, one, two, c1, c2)
        left, right = new_left, new_right
    (final,) = call(last_kernel, [(blocks, bf16)], [smem()] + [vmem()] * 10, "last")(
        cols, in_vmem(left), in_vmem(right), value16, value32, first32, last32, one, two, c1, c2
    )
    exchanged = lax.all_to_all(final, "comp", split_axis=0, concat_axis=0, tiled=True)
    return source_terms(exchanged.reshape(n * rows, width), quad_one, quad_two)


def solution(mesh):
    in_specs = (
        P("comp", "dom"),
        P("comp"),
        P("comp"),
        P("dom", None, None, None),
        P("dom", None, None, None),
        P("dom", None),
        P(),
        P(),
    )
    out_specs = P("dom", "comp", None)
    return jax.shard_map(
        per_device, mesh=mesh, in_specs=in_specs, out_specs=out_specs, check_vma=False
    )
```

```python
import jax
import jax.numpy as jnp
from jax import lax
from jax.experimental import pallas as pl
from jax.experimental.pallas import tpu as pltpu
from jax.sharding import PartitionSpec as P

SUBSTEPS = 4
KEEP = 0.25


def in_vmem(x):
    return pltpu.with_memory_space_constraint(x, pltpu.VMEM)


def in_hbm(x):
    return pltpu.with_memory_space_constraint(x, pltpu.HBM)


def vmem():
    return pl.BlockSpec(memory_space=pltpu.VMEM)


def smem():
    return pl.BlockSpec(memory_space=pltpu.SMEM)


def hbm():
    return pl.BlockSpec(memory_space=pltpu.HBM)


def call(body, outs, in_specs, name, scratch=(), limit=4 << 20):
    return pl.pallas_call(
        body,
        out_shape=[space(shape, dtype) for space, shape, dtype in outs],
        in_specs=in_specs,
        out_specs=[smem() if space is pltpu.SMEM else vmem() for space, _, _ in outs],
        scratch_shapes=list(scratch),
        compiler_params=pltpu.CompilerParams(vmem_limit_bytes=limit),
        name=name,
    )


def row_update(b, chosen, before, after, value, one, two, coef_one, coef_two):
    width = value.shape[1]
    gathered = jnp.concatenate([chosen, before, after], axis=1)
    both = jnp.concatenate([one, two], axis=1)
    flow = jnp.dot(gathered, both, preferred_element_type=jnp.float32)
    moved = value + coef_one * flow[:, :width] + coef_two * flow[:, width:]
    return jnp.maximum(moved, KEEP * value)


def chosen_block(e, left, right, blocks_ref):
    n = blocks_ref.shape[0]
    inner = blocks_ref[jnp.clip(e - 1, 0, n - 1)]
    return jnp.where(e == 0, left, jnp.where(e == n + 1, right, inner))


def edge_kernel(cols, left_ref, right_ref, blocks_ref, first_ref, last_ref, one_ref, two_ref, c1_ref, c2_ref, *outs):
    last16, first16, last32, first32 = outs
    n, rows, width = blocks_ref.shape
    left, right = left_ref[...], right_ref[...]
    c1, c2 = c1_ref[...], c2_ref[...]
    for b, value_ref, out16, out32 in ((0, first_ref, first16, first32), (n - 1, last_ref, last16, last32)):
        new = row_update(
            b,
            chosen_block(cols[0, b], left, right, blocks_ref),
            left if b == 0 else blocks_ref[b - 1],
            right if b == n - 1 else blocks_ref[b + 1],
            value_ref[...],
            one_ref[b].reshape(-1, width),
            two_ref[b].reshape(-1, width),
            c1,
            c2,
        )
        out32[...] = new
        out16[...] = new.astype(jnp.bfloat16)


def inner_kernel(cols, left_ref, right_ref, blocks_ref, field_ref, first16, last16, one_ref, two_ref, c1_ref, c2_ref, *outs):
    out16, out32 = outs
    n, rows, width = blocks_ref.shape
    left, right = left_ref[...], right_ref[...]
    c1, c2 = c1_ref[...], c2_ref[...]
    out16[0] = first16[...]
    out16[n - 1] = last16[...]
    for b in range(1, n - 1):
        new = row_update(
            b,
            chosen_block(cols[0, b], left, right, blocks_ref),
            blocks_ref[b - 1],
            blocks_ref[b + 1],
            field_ref[b],
            one_ref[b].reshape(-1, width),
            two_ref[b].reshape(-1, width),
            c1,
            c2,
        )
        out32[b] = new
        out16[b] = new.astype(jnp.bfloat16)


def last_kernel(cols, left_ref, right_ref, blocks_ref, field_ref, first_ref, last_ref, one_ref, two_ref, c1_ref, c2_ref, *outs):
    (out16,) = outs
    n, rows, width = blocks_ref.shape
    left, right = left_ref[...], right_ref[...]
    c1, c2 = c1_ref[...], c2_ref[...]
    for b in range(n):
        value = first_ref[...] if b == 0 else last_ref[...] if b == n - 1 else field_ref[b]
        new = row_update(
            b,
            chosen_block(cols[0, b], left, right, blocks_ref),
            left if b == 0 else blocks_ref[b - 1],
            right if b == n - 1 else blocks_ref[b + 1],
            value,
            one_ref[b].reshape(-1, width),
            two_ref[b].reshape(-1, width),
            c1,
            c2,
        )
        out16[b] = new.astype(jnp.bfloat16)


def begin_kernel(action_ref, last16, first16, buffers, sems):
    width = first16.shape[1]
    cells = action_ref.shape[1]
    copies = [
        pltpu.make_async_copy(action_ref.at[:, pl.ds(cells - width, width)], buffers.at[0], sems.at[0]),
        pltpu.make_async_copy(action_ref.at[:, pl.ds(0, width)], buffers.at[1], sems.at[1]),
    ]
    for copy in copies:
        copy.start()
    for copy, out, i in zip(copies, (last16, first16), (0, 1)):
        copy.wait()
        out[...] = buffers[i].astype(jnp.bfloat16)


def load_kernel(action_ref, coef_one_hbm, coef_two_hbm, two_hbm, cols_hbm, *refs):
    cols, out16, out32, first32, last32, two, c1, c2, coefs, sems = refs
    n, rows, width = out16.shape
    small = [
        pltpu.make_async_copy(coef_one_hbm, coefs.at[0], sems.at[n]),
        pltpu.make_async_copy(coef_two_hbm, coefs.at[1], sems.at[n + 1]),
        pltpu.make_async_copy(cols_hbm, cols, sems.at[n + 2]),
    ]
    blocks = [
        pltpu.make_async_copy(action_ref.at[:, pl.ds(b * width, width)], out32.at[b], sems.at[b])
        for b in range(n)
    ]
    weights = pltpu.make_async_copy(two_hbm, two, sems.at[n + 3])
    for copy in small + blocks + [weights]:
        copy.start()
    for copy in small:
        copy.wait()
    c1[...] = jnp.broadcast_to(coefs[0], (width, rows)).T
    c2[...] = jnp.broadcast_to(coefs[1], (width, rows)).T
    for b in range(n):
        blocks[b].wait()
        out16[b] = out32[b].astype(jnp.bfloat16)
    first32[...] = out32[0]
    last32[...] = out32[n - 1]
    weights.wait()


def source_kernel(cells_ref, one_ref, two_ref, out_hbm, buffers, sems):
    steps, _, tile = buffers.shape
    cells = cells_ref[...].T
    copies = []
    for i in range(steps):
        at = slice(i * tile, (i + 1) * tile)
        own = cells[:, at].astype(jnp.float32)
        first = jnp.dot(cells, one_ref[:, at], preferred_element_type=jnp.float32)
        second = jnp.dot(cells, two_ref[:, at], preferred_element_type=jnp.float32)
        buffers[i] = own + 0.5 * (first * own - second * own * own)
        copies.append(pltpu.make_async_copy(buffers.at[i], out_hbm.at[0, :, pl.ds(i * tile, tile)], sems.at[i]))
        copies[-1].start()
    for copy in copies:
        copy.wait()


def source_terms(exchanged, quad_one, quad_two):
    comps, cells = exchanged.shape
    tile = 384
    steps = comps // tile
    return pl.pallas_call(
        source_kernel,
        out_shape=jax.ShapeDtypeStruct((1, cells, comps), jnp.float32),
        in_specs=[vmem()] * 3,
        out_specs=hbm(),
        scratch_shapes=[
            pltpu.VMEM((steps, cells, tile), jnp.float32),
            pltpu.SemaphoreType.DMA((steps,)),
        ],
        compiler_params=pltpu.CompilerParams(vmem_limit_bytes=8 << 20),
        name="source_terms",
    )(in_vmem(exchanged), in_vmem(quad_one), in_vmem(quad_two))


def per_device(
    action, coef_one, coef_two, transport_one, transport_two, block_cols, quad_one, quad_two
):
    rows, cells_dev = action.shape
    n, nnz, width, _ = transport_one.shape
    dom = lax.axis_size("dom")
    up = [(i, i + 1) for i in range(dom - 1)]
    down = [(i + 1, i) for i in range(dom - 1)]
    bf16, f32 = jnp.bfloat16, jnp.float32
    block, blocks, weights = (rows, width), (n, rows, width), (n, nnz, width, width)

    vm = lambda shape, dtype: (pltpu.VMEM, shape, dtype)
    last, first = call(
        begin_kernel,
        [vm(block, bf16), vm(block, bf16)],
        [hbm()],
        "begin",
        [pltpu.VMEM((2, rows, width), f32), pltpu.SemaphoreType.DMA((2,))],
    )(in_hbm(action))
    left = lax.ppermute(last, "dom", up)
    right = lax.ppermute(first, "dom", down)
    cols, value16, value32, first32, last32, two, c1, c2 = call(
        load_kernel,
        [(pltpu.SMEM, (nnz, n), jnp.int32), vm(blocks, bf16), vm(blocks, f32), vm(block, f32), vm(block, f32)]
        + [vm(weights, bf16), vm(block, f32), vm(block, f32)],
        [hbm()] * 5,
        "load",
        [pltpu.VMEM((2, 1, rows), f32), pltpu.SemaphoreType.DMA((n + 4,))],
    )(
        in_hbm(action),
        in_hbm(coef_one.reshape(1, rows)),
        in_hbm(coef_two.reshape(1, rows)),
        in_hbm(transport_two),
        in_hbm(block_cols.T),
    )
    one = in_vmem(transport_one)
    for substep in range(SUBSTEPS - 1):
        last, first, last32, first32 = call(
            edge_kernel,
            [vm(block, bf16), vm(block, bf16), vm(block, f32), vm(block, f32)],
            [smem()] + [vmem()] * 9,
            "edges",
        )(cols, in_vmem(left), in_vmem(right), value16, first32, last32, one, two, c1, c2)
        new_left = lax.ppermute(last, "dom", up)
        new_right = lax.ppermute(first, "dom", down)
        value16, value32 = call(
            inner_kernel, [vm(blocks, bf16), vm(blocks, f32)], [smem()] + [vmem()] * 10, "inner"
        )(cols, in_vmem(left), in_vmem(right), value16, value32, first, last, one, two, c1, c2)
        left, right = new_left, new_right
    (final,) = call(last_kernel, [vm(blocks, bf16)], [smem()] + [vmem()] * 10, "last")(
        cols, in_vmem(left), in_vmem(right), value16, value32, first32, last32, one, two, c1, c2
    )
    exchanged = lax.all_to_all(final, "comp", split_axis=0, concat_axis=0, tiled=True)
    return source_terms(exchanged.reshape(n * rows, width), quad_one, quad_two)


def solution(mesh):
    in_specs = (
        P("comp", "dom"),
        P("comp"),
        P("comp"),
        P("dom", None, None, None),
        P("dom", None, None, None),
        P("dom", None),
        P(),
        P(),
    )
    out_specs = P("dom", "comp", None)
    return jax.shard_map(
        per_device, mesh=mesh, in_specs=in_specs, out_specs=out_specs, check_vma=False
    )
```

```python
import jax
import jax.numpy as jnp
from jax import lax
from jax.experimental import pallas as pl
from jax.experimental.pallas import tpu as pltpu
from jax.sharding import PartitionSpec as P

SUBSTEPS = 4
KEEP = 0.25


def in_vmem(x):
    return pltpu.with_memory_space_constraint(x, pltpu.VMEM)


def in_hbm(x):
    return pltpu.with_memory_space_constraint(x, pltpu.HBM)


def vmem():
    return pl.BlockSpec(memory_space=pltpu.VMEM)


def smem():
    return pl.BlockSpec(memory_space=pltpu.SMEM)


def hbm():
    return pl.BlockSpec(memory_space=pltpu.HBM)


def call(body, outs, in_specs, name, scratch=(), limit=4 << 20, aliases={}):
    return pl.pallas_call(
        body,
        out_shape=[space(shape, dtype) for space, shape, dtype in outs],
        in_specs=in_specs,
        out_specs=[smem() if space is pltpu.SMEM else vmem() for space, _, _ in outs],
        scratch_shapes=list(scratch),
        input_output_aliases=aliases,
        compiler_params=pltpu.CompilerParams(vmem_limit_bytes=limit),
        name=name,
    )


def row_update(chosen, before, after, value, one, two, coef_one, coef_two):
    width = value.shape[1]
    gathered = jnp.concatenate([chosen, before, after], axis=1)
    both = jnp.concatenate([one, two], axis=1)
    flow = jnp.dot(gathered, both, preferred_element_type=jnp.float32)
    moved = value + coef_one * flow[:, :width] + coef_two * flow[:, width:]
    return jnp.maximum(moved, KEEP * value)


def chosen_block(e, left, right, blocks_ref):
    n = blocks_ref.shape[0]
    inner = blocks_ref[jnp.clip(e - 1, 0, n - 1)]
    return jnp.where(e == 0, left, jnp.where(e == n + 1, right, inner))


def edge_kernel(cols, left_ref, right_ref, blocks_ref, first_ref, last_ref, one_ref, two_ref, c1_ref, c2_ref, *outs):
    last16, first16, last32, first32 = outs
    n, rows, width = blocks_ref.shape
    left, right = left_ref[...], right_ref[...]
    c1, c2 = c1_ref[...], c2_ref[...]
    for b, value_ref, out16, out32 in ((0, first_ref, first16, first32), (n - 1, last_ref, last16, last32)):
        new = row_update(
            chosen_block(cols[0, b], left, right, blocks_ref),
            left if b == 0 else blocks_ref[b - 1],
            right if b == n - 1 else blocks_ref[b + 1],
            value_ref[...],
            one_ref[b].reshape(-1, width),
            two_ref[b].reshape(-1, width),
            c1,
            c2,
        )
        out32[...] = new
        out16[...] = new.astype(jnp.bfloat16)


def inner_kernel(cols, left_ref, right_ref, blocks_ref, field_ref, first16, last16, one_ref, two_ref, c1_ref, c2_ref, *outs):
    out16, out32 = outs
    n, rows, width = blocks_ref.shape
    left, right = left_ref[...], right_ref[...]
    c1, c2 = c1_ref[...], c2_ref[...]
    out16[0] = first16[...]
    out16[n - 1] = last16[...]
    for b in range(1, n - 1):
        new = row_update(
            chosen_block(cols[0, b], left, right, blocks_ref),
            blocks_ref[b - 1],
            blocks_ref[b + 1],
            field_ref[b],
            one_ref[b].reshape(-1, width),
            two_ref[b].reshape(-1, width),
            c1,
            c2,
        )
        out32[b] = new
        out16[b] = new.astype(jnp.bfloat16)


def last_inner_kernel(cols, blocks_ref, field_ref, one_ref, two_ref, c1_ref, c2_ref, out16):
    n, rows, width = blocks_ref.shape
    c1, c2 = c1_ref[...], c2_ref[...]
    for b in range(1, n - 1):
        new = row_update(
            blocks_ref[jnp.clip(cols[0, b] - 1, 0, n - 1)],
            blocks_ref[b - 1],
            blocks_ref[b + 1],
            field_ref[b],
            one_ref[b].reshape(-1, width),
            two_ref[b].reshape(-1, width),
            c1,
            c2,
        )
        out16[b] = new.astype(jnp.bfloat16)


def last_edge_kernel(cols, left_ref, right_ref, blocks_ref, field_ref, first_ref, last_ref, one_ref, two_ref, c1_ref, c2_ref, inner_ref, out16):
    n, rows, width = blocks_ref.shape
    left, right = left_ref[...], right_ref[...]
    c1, c2 = c1_ref[...], c2_ref[...]

    def one_row(b, value):
        new = row_update(
            chosen_block(cols[0, b], left, right, blocks_ref),
            left if b == 0 else blocks_ref[b - 1],
            right if b == n - 1 else blocks_ref[b + 1],
            value,
            one_ref[b].reshape(-1, width),
            two_ref[b].reshape(-1, width),
            c1,
            c2,
        )
        out16[b] = new.astype(jnp.bfloat16)

    one_row(0, first_ref[...])
    one_row(n - 1, last_ref[...])
    for b in range(1, n - 1):
        @pl.when((cols[0, b] == 0) | (cols[0, b] == n + 1))
        def _(b=b):
            one_row(b, field_ref[b])


def begin_kernel(action_ref, last16, first16, buffers, sems):
    width = first16.shape[1]
    cells = action_ref.shape[1]
    copies = [
        pltpu.make_async_copy(action_ref.at[:, pl.ds(cells - width, width)], buffers.at[0], sems.at[0]),
        pltpu.make_async_copy(action_ref.at[:, pl.ds(0, width)], buffers.at[1], sems.at[1]),
    ]
    for copy in copies:
        copy.start()
    for copy, out, i in zip(copies, (last16, first16), (0, 1)):
        copy.wait()
        out[...] = buffers[i].astype(jnp.bfloat16)


def load_kernel(action_ref, coef_one_hbm, coef_two_hbm, two_hbm, cols_hbm, *refs):
    cols, out16, out32, first32, last32, two, c1, c2, coefs, sems = refs
    n, rows, width = out16.shape
    small = [
        pltpu.make_async_copy(coef_one_hbm, coefs.at[0], sems.at[n]),
        pltpu.make_async_copy(coef_two_hbm, coefs.at[1], sems.at[n + 1]),
        pltpu.make_async_copy(cols_hbm, cols, sems.at[n + 2]),
    ]
    blocks = [
        pltpu.make_async_copy(action_ref.at[:, pl.ds(b * width, width)], out32.at[b], sems.at[b])
        for b in range(n)
    ]
    weights = pltpu.make_async_copy(two_hbm, two, sems.at[n + 3])
    for copy in small + blocks + [weights]:
        copy.start()
    for copy in small:
        copy.wait()
    c1[...] = jnp.broadcast_to(coefs[0], (width, rows)).T
    c2[...] = jnp.broadcast_to(coefs[1], (width, rows)).T
    for b in range(n):
        blocks[b].wait()
        out16[b] = out32[b].astype(jnp.bfloat16)
    first32[...] = out32[0]
    last32[...] = out32[n - 1]
    weights.wait()


def source_kernel(cells_ref, one_ref, two_ref, out_hbm, buffers, sems):
    steps, _, tile = buffers.shape
    cells = cells_ref[...].T
    copies = []
    for i in range(steps):
        at = slice(i * tile, (i + 1) * tile)
        own = cells[:, at].astype(jnp.float32)
        quads = jnp.concatenate([one_ref[:, at], two_ref[:, at]], axis=1)
        both = jnp.dot(cells, quads, preferred_element_type=jnp.float32)
        first, second = both[:, :tile], both[:, tile:]
        buffers[i] = own + 0.5 * (first * own - second * own * own)
        copies.append(pltpu.make_async_copy(buffers.at[i], out_hbm.at[0, :, pl.ds(i * tile, tile)], sems.at[i]))
        copies[-1].start()
    for copy in copies:
        copy.wait()


def source_terms(exchanged, quad_one, quad_two):
    comps, cells = exchanged.shape
    tile = 128
    steps = comps // tile
    return pl.pallas_call(
        source_kernel,
        out_shape=jax.ShapeDtypeStruct((1, cells, comps), jnp.float32),
        in_specs=[vmem()] * 3,
        out_specs=hbm(),
        scratch_shapes=[
            pltpu.VMEM((steps, cells, tile), jnp.float32),
            pltpu.SemaphoreType.DMA((steps,)),
        ],
        compiler_params=pltpu.CompilerParams(vmem_limit_bytes=8 << 20),
        name="source_terms",
    )(in_vmem(exchanged), in_vmem(quad_one), in_vmem(quad_two))


def per_device(
    action, coef_one, coef_two, transport_one, transport_two, block_cols, quad_one, quad_two
):
    rows, cells_dev = action.shape
    n, nnz, width, _ = transport_one.shape
    dom = lax.axis_size("dom")
    up = [(i, i + 1) for i in range(dom - 1)]
    down = [(i + 1, i) for i in range(dom - 1)]
    bf16, f32 = jnp.bfloat16, jnp.float32
    block, blocks, weights = (rows, width), (n, rows, width), (n, nnz, width, width)

    vm = lambda shape, dtype: (pltpu.VMEM, shape, dtype)
    last, first = call(
        begin_kernel,
        [vm(block, bf16), vm(block, bf16)],
        [hbm()],
        "begin",
        [pltpu.VMEM((2, rows, width), f32), pltpu.SemaphoreType.DMA((2,))],
    )(in_hbm(action))
    left = lax.ppermute(last, "dom", up)
    right = lax.ppermute(first, "dom", down)
    cols, value16, value32, first32, last32, two, c1, c2 = call(
        load_kernel,
        [(pltpu.SMEM, (nnz, n), jnp.int32), vm(blocks, bf16), vm(blocks, f32), vm(block, f32), vm(block, f32)]
        + [vm(weights, bf16), vm(block, f32), vm(block, f32)],
        [hbm()] * 5,
        "load",
        [pltpu.VMEM((2, 1, rows), f32), pltpu.SemaphoreType.DMA((n + 4,))],
    )(
        in_hbm(action),
        in_hbm(coef_one.reshape(1, rows)),
        in_hbm(coef_two.reshape(1, rows)),
        in_hbm(transport_two),
        in_hbm(block_cols.T),
    )
    one = in_vmem(transport_one)
    for substep in range(SUBSTEPS - 1):
        last, first, last32, first32 = call(
            edge_kernel,
            [vm(block, bf16), vm(block, bf16), vm(block, f32), vm(block, f32)],
            [smem()] + [vmem()] * 9,
            "edges",
        )(cols, in_vmem(left), in_vmem(right), value16, first32, last32, one, two, c1, c2)
        new_left = lax.ppermute(last, "dom", up)
        new_right = lax.ppermute(first, "dom", down)
        value16, value32 = call(
            inner_kernel, [vm(blocks, bf16), vm(blocks, f32)], [smem()] + [vmem()] * 10, "inner"
        )(cols, in_vmem(left), in_vmem(right), value16, value32, first, last, one, two, c1, c2)
        left, right = new_left, new_right
    (final,) = call(last_inner_kernel, [vm(blocks, bf16)], [smem()] + [vmem()] * 6, "last_inner")(
        cols, value16, value32, one, two, c1, c2
    )
    (final,) = call(
        last_edge_kernel, [vm(blocks, bf16)], [smem()] + [vmem()] * 11, "last_edge", aliases={11: 0}
    )(cols, in_vmem(left), in_vmem(right), value16, value32, first32, last32, one, two, c1, c2, final)
    exchanged = lax.all_to_all(final, "comp", split_axis=0, concat_axis=0, tiled=True)
    return source_terms(exchanged.reshape(n * rows, width), quad_one, quad_two)


def solution(mesh):
    in_specs = (
        P("comp", "dom"),
        P("comp"),
        P("comp"),
        P("dom", None, None, None),
        P("dom", None, None, None),
        P("dom", None),
        P(),
        P(),
    )
    out_specs = P("dom", "comp", None)
    return jax.shard_map(
        per_device, mesh=mesh, in_specs=in_specs, out_specs=out_specs, check_vma=False
    )
```

```python
import jax
import jax.numpy as jnp
from jax import lax
from jax.experimental import pallas as pl
from jax.experimental.pallas import tpu as pltpu
from jax.sharding import PartitionSpec as P

SUBSTEPS = 4
KEEP = 0.25
CHAIN = 12
ROUND = 3


def in_vmem(x):
    return pltpu.with_memory_space_constraint(x, pltpu.VMEM)


def in_hbm(x):
    return pltpu.with_memory_space_constraint(x, pltpu.HBM)


def vmem():
    return pl.BlockSpec(memory_space=pltpu.VMEM)


def smem():
    return pl.BlockSpec(memory_space=pltpu.SMEM)


def hbm():
    return pl.BlockSpec(memory_space=pltpu.HBM)


def call(body, outs, in_specs, name, scratch=(), limit=4 << 20, aliases={}):
    return pl.pallas_call(
        body,
        out_shape=[space(shape, dtype) for space, shape, dtype in outs],
        in_specs=in_specs,
        out_specs=[smem() if space is pltpu.SMEM else vmem() for space, _, _ in outs],
        scratch_shapes=list(scratch),
        input_output_aliases=aliases,
        compiler_params=pltpu.CompilerParams(vmem_limit_bytes=limit),
        name=name,
    )


def row_update(chosen, before, after, value, one, two, coef_one, coef_two):
    width = value.shape[1]
    gathered = jnp.concatenate([chosen, before, after], axis=1)
    both = jnp.concatenate([one, two], axis=1)
    flow = jnp.dot(gathered, both, preferred_element_type=jnp.float32)
    moved = value + coef_one * flow[:, :width] + coef_two * flow[:, width:]
    return jnp.maximum(moved, KEEP * value)


def exchange_of(edge):
    place = edge % CHAIN
    return jnp.where(place == CHAIN - 1, 1, jnp.where(place == CHAIN - 2, 2, place % 2))


def pairs_of(exchange, dom):
    def carries(edge):
        place = edge % CHAIN
        return (1 if place == CHAIN - 1 else 2 if place == CHAIN - 2 else place % 2) == exchange

    edges = [d for d in range(dom - 1) if carries(d)]
    return [p for d in edges for p in ((d, d + 1), (d + 1, d))]


def sides():
    own = lax.axis_index("dom")
    return exchange_of(own + CHAIN - 1), exchange_of(own)


def pick(which, parts):
    return jnp.where(which == 0, parts[0], jnp.where(which == 1, parts[1], parts[2]))


def halos(received):
    parts = [r[...] for r in received]
    to_left, to_right = sides()
    return pick(to_left, parts), pick(to_right, parts)


def send(outs, first, last):
    to_left, _ = sides()
    for exchange, out in enumerate(outs):
        out[...] = jnp.where(to_left == exchange, first, last)


def chosen_block(e, left, right, blocks_ref):
    n = blocks_ref.shape[0]
    inner = blocks_ref[jnp.clip(e - 1, 0, n - 1)]
    return jnp.where(e == 0, left, jnp.where(e == n + 1, right, inner))


def edge_rows(cols, left, right, blocks_ref, first, last, one_ref, two_ref, c1, c2):
    n, rows, width = blocks_ref.shape
    return [
        row_update(
            chosen_block(cols[0, b], left, right, blocks_ref),
            left if b == 0 else blocks_ref[b - 1],
            right if b == n - 1 else blocks_ref[b + 1],
            value,
            one_ref[b].reshape(-1, width),
            two_ref[b].reshape(-1, width),
            c1,
            c2,
        )
        for b, value in ((0, first), (n - 1, last))
    ]


def edge_kernel(cols, in0, in1, in2, blocks_ref, ends_ref, one_ref, two_ref, c1_ref, c2_ref, *outs):
    out0, out1, out2, ends16, ends32 = outs
    left, right = halos((in0, in1, in2))
    first, last = edge_rows(
        cols, left, right, blocks_ref, ends_ref[0], ends_ref[1], one_ref, two_ref, c1_ref[...], c2_ref[...]
    )
    ends32[0], ends32[1] = first, last
    first, last = first.astype(jnp.bfloat16), last.astype(jnp.bfloat16)
    ends16[0], ends16[1] = first, last
    send((out0, out1, out2), first, last)


def inner_kernel(cols, in0, in1, in2, blocks_ref, field_ref, ends16, one_ref, two_ref, c1_ref, c2_ref, *outs):
    out16, out32 = outs
    n, rows, width = blocks_ref.shape
    left, right = halos((in0, in1, in2))
    c1, c2 = c1_ref[...], c2_ref[...]
    out16[0] = ends16[0]
    out16[n - 1] = ends16[1]
    for b in range(1, n - 1):
        new = row_update(
            chosen_block(cols[0, b], left, right, blocks_ref),
            blocks_ref[b - 1],
            blocks_ref[b + 1],
            field_ref[b],
            one_ref[b].reshape(-1, width),
            two_ref[b].reshape(-1, width),
            c1,
            c2,
        )
        out32[b] = new
        out16[b] = new.astype(jnp.bfloat16)


def last_inner_kernel(cols, blocks_ref, field_ref, one_ref, two_ref, c1_ref, c2_ref, out16):
    n, rows, width = blocks_ref.shape
    c1, c2 = c1_ref[...], c2_ref[...]
    for b in range(1, n - 1):
        new = row_update(
            blocks_ref[jnp.clip(cols[0, b] - 1, 0, n - 1)],
            blocks_ref[b - 1],
            blocks_ref[b + 1],
            field_ref[b],
            one_ref[b].reshape(-1, width),
            two_ref[b].reshape(-1, width),
            c1,
            c2,
        )
        out16[b] = new.astype(jnp.bfloat16)


def last_edge_kernel(cols, todo, in0, in1, in2, blocks_ref, field_ref, ends_ref, one_ref, two_ref, c1_ref, c2_ref, inner_ref, out16):
    n, rows, width = blocks_ref.shape
    left, right = halos((in0, in1, in2))
    c1, c2 = c1_ref[...], c2_ref[...]

    def again(b):
        return row_update(
            chosen_block(cols[0, b], left, right, blocks_ref),
            blocks_ref[b - 1],
            blocks_ref[b + 1],
            field_ref[b],
            one_ref[b].reshape(-1, width),
            two_ref[b].reshape(-1, width),
            c1,
            c2,
        ).astype(jnp.bfloat16)

    first, last = edge_rows(
        cols, left, right, blocks_ref, ends_ref[0], ends_ref[1], one_ref, two_ref, c1, c2
    )
    at = [todo[0, i] for i in range(ROUND)]
    new = [again(b) for b in at]
    out16[0] = first.astype(jnp.bfloat16)
    out16[n - 1] = last.astype(jnp.bfloat16)
    for b, value in zip(at, new):
        out16[b] = value

    @pl.when(todo[0, n - 1] > ROUND)
    def _():
        @pl.loop(ROUND, todo[0, n - 1])
        def _(i):
            b = todo[0, i]
            out16[b] = again(b)


def begin_kernel(action_ref, out0, out1, out2, buffers, sems):
    width = out0.shape[1]
    cells = action_ref.shape[1]
    copies = [
        pltpu.make_async_copy(action_ref.at[:, pl.ds(at, width)], buffers.at[i], sems.at[i])
        for i, at in enumerate((0, cells - width))
    ]
    for copy in copies:
        copy.start()
    for copy in copies:
        copy.wait()
    send((out0, out1, out2), buffers[0].astype(jnp.bfloat16), buffers[1].astype(jnp.bfloat16))


def load_kernel(action_ref, coef_one_hbm, coef_two_hbm, two_hbm, cols_hbm, *refs):
    cols, todo, out16, out32, ends32, two, c1, c2, coefs, sems = refs
    n, rows, width = out16.shape
    small = [
        pltpu.make_async_copy(cols_hbm, cols, sems.at[n + 2]),
        pltpu.make_async_copy(coef_one_hbm, coefs.at[0], sems.at[n]),
        pltpu.make_async_copy(coef_two_hbm, coefs.at[1], sems.at[n + 1]),
    ]
    blocks = [
        pltpu.make_async_copy(action_ref.at[:, pl.ds(b * width, width)], out32.at[b], sems.at[b])
        for b in range(n)
    ]
    weights = pltpu.make_async_copy(two_hbm, two, sems.at[n + 3])
    for copy in small + blocks + [weights]:
        copy.start()
    for copy in small:
        copy.wait()
    for i in range(n):
        todo[0, i] = 1
    count = jnp.int32(0)
    for b in range(1, n - 1):
        e = cols[0, b]
        reads_halo = (e == 0) | (e == n + 1)

        @pl.when(reads_halo)
        def _(b=b, count=count):
            todo[0, count] = b

        count = count + reads_halo.astype(jnp.int32)
    todo[0, n - 1] = count
    c1[...] = jnp.broadcast_to(coefs[0], (width, rows)).T
    c2[...] = jnp.broadcast_to(coefs[1], (width, rows)).T
    for b in range(n):
        blocks[b].wait()
        out16[b] = out32[b].astype(jnp.bfloat16)
    ends32[0] = out32[0]
    ends32[1] = out32[n - 1]
    weights.wait()


def source_kernel(cells_ref, one_ref, two_ref, out_hbm, buffers, sems):
    steps, _, tile = buffers.shape
    cells = cells_ref[...].T
    copies = []
    for i in range(steps):
        at = slice(i * tile, (i + 1) * tile)
        own = cells[:, at].astype(jnp.float32)
        quads = jnp.concatenate([one_ref[:, at], two_ref[:, at]], axis=1)
        both = jnp.dot(cells, quads, preferred_element_type=jnp.float32)
        first, second = both[:, :tile], both[:, tile:]
        buffers[i] = own + 0.5 * (first * own - second * own * own)
        copies.append(pltpu.make_async_copy(buffers.at[i], out_hbm.at[0, :, pl.ds(i * tile, tile)], sems.at[i]))
        copies[-1].start()
    for copy in copies:
        copy.wait()


def source_terms(exchanged, quad_one, quad_two):
    comps, cells = exchanged.shape
    tile = 128
    steps = comps // tile
    return pl.pallas_call(
        source_kernel,
        out_shape=jax.ShapeDtypeStruct((1, cells, comps), jnp.float32),
        in_specs=[vmem()] * 3,
        out_specs=hbm(),
        scratch_shapes=[
            pltpu.VMEM((steps, cells, tile), jnp.float32),
            pltpu.SemaphoreType.DMA((steps,)),
        ],
        compiler_params=pltpu.CompilerParams(vmem_limit_bytes=8 << 20),
        name="source_terms",
    )(in_vmem(exchanged), in_vmem(quad_one), in_vmem(quad_two))


def per_device(
    action, coef_one, coef_two, transport_one, transport_two, block_cols, quad_one, quad_two
):
    rows, cells_dev = action.shape
    n, nnz, width, _ = transport_one.shape
    dom = lax.axis_size("dom")
    bf16, f32 = jnp.bfloat16, jnp.float32
    block, blocks, ends, weights = (rows, width), (n, rows, width), (2, rows, width), (n, nnz, width, width)
    vm = lambda shape, dtype: (pltpu.VMEM, shape, dtype)
    sm = lambda shape: (pltpu.SMEM, shape, jnp.int32)
    exchange = lambda parts: [
        in_vmem(lax.ppermute(x, "dom", pairs_of(i, dom))) for i, x in enumerate(parts)
    ]

    received = exchange(
        call(
            begin_kernel,
            [vm(block, bf16)] * 3,
            [hbm()],
            "begin",
            [pltpu.VMEM((2, rows, width), f32), pltpu.SemaphoreType.DMA((2,))],
        )(in_hbm(action))
    )
    cols, todo, value16, value32, ends32, two, c1, c2 = call(
        load_kernel,
        [sm((nnz, n)), sm((1, n)), vm(blocks, bf16), vm(blocks, f32), vm(ends, f32)]
        + [vm(weights, bf16), vm(block, f32), vm(block, f32)],
        [hbm()] * 5,
        "load",
        [pltpu.VMEM((2, 1, rows), f32), pltpu.SemaphoreType.DMA((n + 4,))],
    )(
        in_hbm(action),
        in_hbm(coef_one.reshape(1, rows)),
        in_hbm(coef_two.reshape(1, rows)),
        in_hbm(transport_two),
        in_hbm(block_cols.T),
    )
    one = in_vmem(transport_one)
    for substep in range(SUBSTEPS - 1):
        *parts, ends16, ends32 = call(
            edge_kernel,
            [vm(block, bf16)] * 3 + [vm(ends, bf16), vm(ends, f32)],
            [smem()] + [vmem()] * 9,
            "edges",
        )(cols, *received, value16, ends32, one, two, c1, c2)
        new_received = exchange(parts)
        value16, value32 = call(
            inner_kernel, [vm(blocks, bf16), vm(blocks, f32)], [smem()] + [vmem()] * 10, "inner"
        )(cols, *received, value16, value32, ends16, one, two, c1, c2)
        received = new_received
    (final,) = call(last_inner_kernel, [vm(blocks, bf16)], [smem()] + [vmem()] * 6, "last_inner")(
        cols, value16, value32, one, two, c1, c2
    )
    (final,) = call(
        last_edge_kernel, [vm(blocks, bf16)], [smem()] * 2 + [vmem()] * 11, "last_edge", aliases={12: 0}
    )(cols, todo, *received, value16, value32, ends32, one, two, c1, c2, final)
    exchanged = lax.all_to_all(final, "comp", split_axis=0, concat_axis=0, tiled=True)
    return source_terms(exchanged.reshape(n * rows, width), quad_one, quad_two)


def solution(mesh):
    in_specs = (
        P("comp", "dom"),
        P("comp"),
        P("comp"),
        P("dom", None, None, None),
        P("dom", None, None, None),
        P("dom", None),
        P(),
        P(),
    )
    out_specs = P("dom", "comp", None)
    return jax.shard_map(
        per_device, mesh=mesh, in_specs=in_specs, out_specs=out_specs, check_vma=False
    )
```

```python
import jax
import jax.numpy as jnp
from jax import lax
from jax.experimental import pallas as pl
from jax.experimental.pallas import tpu as pltpu
from jax.sharding import PartitionSpec as P

SUBSTEPS = 4
KEEP = 0.25
CHAIN = 12
ROUND = 3


def in_vmem(x):
    return pltpu.with_memory_space_constraint(x, pltpu.VMEM)


def in_hbm(x):
    return pltpu.with_memory_space_constraint(x, pltpu.HBM)


def vmem():
    return pl.BlockSpec(memory_space=pltpu.VMEM)


def smem():
    return pl.BlockSpec(memory_space=pltpu.SMEM)


def hbm():
    return pl.BlockSpec(memory_space=pltpu.HBM)


def call(body, outs, in_specs, name, scratch=(), limit=4 << 20, aliases={}):
    return pl.pallas_call(
        body,
        out_shape=[space(shape, dtype) for space, shape, dtype in outs],
        in_specs=in_specs,
        out_specs=[smem() if space is pltpu.SMEM else vmem() for space, _, _ in outs],
        scratch_shapes=list(scratch),
        input_output_aliases=aliases,
        compiler_params=pltpu.CompilerParams(vmem_limit_bytes=limit),
        name=name,
    )


def row_update(chosen, before, after, value, one, two, coef_one, coef_two):
    width = value.shape[1]
    gathered = jnp.concatenate([chosen, before, after], axis=1)
    both = jnp.concatenate([one, two], axis=1)
    flow = jnp.dot(gathered, both, preferred_element_type=jnp.float32)
    moved = value + coef_one * flow[:, :width] + coef_two * flow[:, width:]
    return jnp.maximum(moved, KEEP * value)


def up_of(edge):
    place = edge % CHAIN
    return 2 * (place < 5) + 1 * (place == 5) + 1 * (place == CHAIN - 1)


def down_of(edge):
    place = edge % CHAIN
    return 1 * (place == 5) + 1 * (place == CHAIN - 1) + 2 * (place > 5) * (place < CHAIN - 1)


def pairs_of(exchange, dom):
    edges = range(dom - 1)
    return [(d, d + 1) for d in edges if up_of(d) == exchange] + [
        (d + 1, d) for d in edges if down_of(d) == exchange
    ]


def pick(which, parts):
    picked = parts[-1]
    for exchange in range(len(parts) - 2, -1, -1):
        picked = jnp.where(which == exchange, parts[exchange], picked)
    return picked


def halos(received):
    parts = [r[...] for r in received]
    own = lax.axis_index("dom")
    return pick(up_of(own + CHAIN - 1), parts), pick(down_of(own), parts)


def send(outs, first, last):
    to_left = down_of(lax.axis_index("dom") + CHAIN - 1)
    for exchange, out in enumerate(outs):
        out[...] = jnp.where(to_left == exchange, first, last)


def chosen_block(e, left, right, blocks_ref):
    n = blocks_ref.shape[0]
    inner = blocks_ref[jnp.clip(e - 1, 0, n - 1)]
    return jnp.where(e == 0, left, jnp.where(e == n + 1, right, inner))


def edge_rows(cols, left, right, blocks_ref, first, last, one_ref, two_ref, c1, c2):
    n, rows, width = blocks_ref.shape
    return [
        row_update(
            chosen_block(cols[0, b], left, right, blocks_ref),
            left if b == 0 else blocks_ref[b - 1],
            right if b == n - 1 else blocks_ref[b + 1],
            value,
            one_ref[b].reshape(-1, width),
            two_ref[b].reshape(-1, width),
            c1,
            c2,
        )
        for b, value in ((0, first), (n - 1, last))
    ]


def edge_kernel(cols, in0, in1, in2, blocks_ref, ends_ref, one_ref, two_ref, c1_ref, c2_ref, *outs):
    out0, out1, out2, ends16, ends32 = outs
    left, right = halos((in0, in1, in2))
    first, last = edge_rows(
        cols, left, right, blocks_ref, ends_ref[0], ends_ref[1], one_ref, two_ref, c1_ref[...], c2_ref[...]
    )
    ends32[0], ends32[1] = first, last
    first, last = first.astype(jnp.bfloat16), last.astype(jnp.bfloat16)
    ends16[0], ends16[1] = first, last
    send((out0, out1, out2), first, last)


def inner_kernel(cols, in0, in1, in2, blocks_ref, field_ref, ends16, one_ref, two_ref, c1_ref, c2_ref, *outs):
    out16, out32 = outs
    n, rows, width = blocks_ref.shape
    left, right = halos((in0, in1, in2))
    c1, c2 = c1_ref[...], c2_ref[...]
    out16[0] = ends16[0]
    out16[n - 1] = ends16[1]
    for b in range(1, n - 1):
        new = row_update(
            chosen_block(cols[0, b], left, right, blocks_ref),
            blocks_ref[b - 1],
            blocks_ref[b + 1],
            field_ref[b],
            one_ref[b].reshape(-1, width),
            two_ref[b].reshape(-1, width),
            c1,
            c2,
        )
        out32[b] = new
        out16[b] = new.astype(jnp.bfloat16)


def last_inner_kernel(cols, blocks_ref, field_ref, one_ref, two_ref, c1_ref, c2_ref, out16):
    n, rows, width = blocks_ref.shape
    c1, c2 = c1_ref[...], c2_ref[...]
    for b in range(1, n - 1):
        new = row_update(
            blocks_ref[jnp.clip(cols[0, b] - 1, 0, n - 1)],
            blocks_ref[b - 1],
            blocks_ref[b + 1],
            field_ref[b],
            one_ref[b].reshape(-1, width),
            two_ref[b].reshape(-1, width),
            c1,
            c2,
        )
        out16[b] = new.astype(jnp.bfloat16)


def last_edge_kernel(cols, todo, in0, in1, in2, blocks_ref, field_ref, ends_ref, one_ref, two_ref, c1_ref, c2_ref, inner_ref, out16):
    n, rows, width = blocks_ref.shape
    left, right = halos((in0, in1, in2))
    c1, c2 = c1_ref[...], c2_ref[...]

    def again(b):
        return row_update(
            chosen_block(cols[0, b], left, right, blocks_ref),
            blocks_ref[b - 1],
            blocks_ref[b + 1],
            field_ref[b],
            one_ref[b].reshape(-1, width),
            two_ref[b].reshape(-1, width),
            c1,
            c2,
        ).astype(jnp.bfloat16)

    first, last = edge_rows(
        cols, left, right, blocks_ref, ends_ref[0], ends_ref[1], one_ref, two_ref, c1, c2
    )
    at = [todo[0, i] for i in range(ROUND)]
    new = [again(b) for b in at]
    out16[0] = first.astype(jnp.bfloat16)
    out16[n - 1] = last.astype(jnp.bfloat16)
    for b, value in zip(at, new):
        out16[b] = value

    @pl.when(todo[0, n - 1] > ROUND)
    def _():
        @pl.loop(ROUND, todo[0, n - 1])
        def _(i):
            b = todo[0, i]
            out16[b] = again(b)


def begin_kernel(action_ref, out0, out1, out2, buffers, sems):
    width = out0.shape[1]
    cells = action_ref.shape[1]
    copies = [
        pltpu.make_async_copy(action_ref.at[:, pl.ds(at, width)], buffers.at[i], sems.at[i])
        for i, at in enumerate((0, cells - width))
    ]
    for copy in copies:
        copy.start()
    for copy in copies:
        copy.wait()
    send((out0, out1, out2), buffers[0].astype(jnp.bfloat16), buffers[1].astype(jnp.bfloat16))


def load_kernel(action_ref, coef_one_hbm, coef_two_hbm, two_hbm, cols_hbm, *refs):
    cols, todo, out16, out32, ends32, two, c1, c2, coefs, sems = refs
    n, rows, width = out16.shape
    small = [
        pltpu.make_async_copy(cols_hbm, cols, sems.at[n + 2]),
        pltpu.make_async_copy(coef_one_hbm, coefs.at[0], sems.at[n]),
        pltpu.make_async_copy(coef_two_hbm, coefs.at[1], sems.at[n + 1]),
    ]
    blocks = [
        pltpu.make_async_copy(action_ref.at[:, pl.ds(b * width, width)], out32.at[b], sems.at[b])
        for b in range(n)
    ]
    weights = pltpu.make_async_copy(two_hbm, two, sems.at[n + 3])
    for copy in small + blocks + [weights]:
        copy.start()
    for copy in small:
        copy.wait()
    for i in range(n):
        todo[0, i] = 1
    count = jnp.int32(0)
    for b in range(1, n - 1):
        e = cols[0, b]
        reads_halo = (e == 0) | (e == n + 1)

        @pl.when(reads_halo)
        def _(b=b, count=count):
            todo[0, count] = b

        count = count + reads_halo.astype(jnp.int32)
    todo[0, n - 1] = count
    c1[...] = jnp.broadcast_to(coefs[0], (width, rows)).T
    c2[...] = jnp.broadcast_to(coefs[1], (width, rows)).T
    for b in range(n):
        blocks[b].wait()
        out16[b] = out32[b].astype(jnp.bfloat16)
    ends32[0] = out32[0]
    ends32[1] = out32[n - 1]
    weights.wait()


def source_kernel(cells_ref, one_ref, two_ref, out_hbm, buffers, sems):
    steps, _, tile = buffers.shape
    cells = cells_ref[...].T
    copies = []
    for i in range(steps):
        at = slice(i * tile, (i + 1) * tile)
        own = cells[:, at].astype(jnp.float32)
        quads = jnp.concatenate([one_ref[:, at], two_ref[:, at]], axis=1)
        both = jnp.dot(cells, quads, preferred_element_type=jnp.float32)
        first, second = both[:, :tile], both[:, tile:]
        buffers[i] = own + 0.5 * (first * own - second * own * own)
        copies.append(pltpu.make_async_copy(buffers.at[i], out_hbm.at[0, :, pl.ds(i * tile, tile)], sems.at[i]))
        copies[-1].start()
    for copy in copies:
        copy.wait()


def source_terms(exchanged, quad_one, quad_two):
    comps, cells = exchanged.shape
    tile = 128
    steps = comps // tile
    return pl.pallas_call(
        source_kernel,
        out_shape=jax.ShapeDtypeStruct((1, cells, comps), jnp.float32),
        in_specs=[vmem()] * 3,
        out_specs=hbm(),
        scratch_shapes=[
            pltpu.VMEM((steps, cells, tile), jnp.float32),
            pltpu.SemaphoreType.DMA((steps,)),
        ],
        compiler_params=pltpu.CompilerParams(vmem_limit_bytes=8 << 20),
        name="source_terms",
    )(in_vmem(exchanged), in_vmem(quad_one), in_vmem(quad_two))


def per_device(
    action, coef_one, coef_two, transport_one, transport_two, block_cols, quad_one, quad_two
):
    rows, cells_dev = action.shape
    n, nnz, width, _ = transport_one.shape
    dom = lax.axis_size("dom")
    bf16, f32 = jnp.bfloat16, jnp.float32
    block, blocks, ends, weights = (rows, width), (n, rows, width), (2, rows, width), (n, nnz, width, width)
    vm = lambda shape, dtype: (pltpu.VMEM, shape, dtype)
    sm = lambda shape: (pltpu.SMEM, shape, jnp.int32)
    exchange = lambda parts: [
        in_vmem(lax.ppermute(x, "dom", pairs_of(i, dom))) for i, x in enumerate(parts)
    ]

    received = exchange(
        call(
            begin_kernel,
            [vm(block, bf16)] * 3,
            [hbm()],
            "begin",
            [pltpu.VMEM((2, rows, width), f32), pltpu.SemaphoreType.DMA((2,))],
        )(in_hbm(action))
    )
    cols, todo, value16, value32, ends32, two, c1, c2 = call(
        load_kernel,
        [sm((nnz, n)), sm((1, n)), vm(blocks, bf16), vm(blocks, f32), vm(ends, f32)]
        + [vm(weights, bf16), vm(block, f32), vm(block, f32)],
        [hbm()] * 5,
        "load",
        [pltpu.VMEM((2, 1, rows), f32), pltpu.SemaphoreType.DMA((n + 4,))],
    )(
        in_hbm(action),
        in_hbm(coef_one.reshape(1, rows)),
        in_hbm(coef_two.reshape(1, rows)),
        in_hbm(transport_two),
        in_hbm(block_cols.T),
    )
    one = in_vmem(transport_one)
    for substep in range(SUBSTEPS - 1):
        *parts, ends16, ends32 = call(
            edge_kernel,
            [vm(block, bf16)] * 3 + [vm(ends, bf16), vm(ends, f32)],
            [smem()] + [vmem()] * 9,
            "edges",
        )(cols, *received, value16, ends32, one, two, c1, c2)
        new_received = exchange(parts)
        value16, value32 = call(
            inner_kernel, [vm(blocks, bf16), vm(blocks, f32)], [smem()] + [vmem()] * 10, "inner"
        )(cols, *received, value16, value32, ends16, one, two, c1, c2)
        received = new_received
    (final,) = call(last_inner_kernel, [vm(blocks, bf16)], [smem()] + [vmem()] * 6, "last_inner")(
        cols, value16, value32, one, two, c1, c2
    )
    (final,) = call(
        last_edge_kernel, [vm(blocks, bf16)], [smem()] * 2 + [vmem()] * 11, "last_edge", aliases={12: 0}
    )(cols, todo, *received, value16, value32, ends32, one, two, c1, c2, final)
    exchanged = lax.all_to_all(final, "comp", split_axis=0, concat_axis=0, tiled=True)
    return source_terms(exchanged.reshape(n * rows, width), quad_one, quad_two)


def solution(mesh):
    in_specs = (
        P("comp", "dom"),
        P("comp"),
        P("comp"),
        P("dom", None, None, None),
        P("dom", None, None, None),
        P("dom", None),
        P(),
        P(),
    )
    out_specs = P("dom", "comp", None)
    return jax.shard_map(
        per_device, mesh=mesh, in_specs=in_specs, out_specs=out_specs, check_vma=False
    )
```

```python
import functools

import jax
import jax.numpy as jnp
from jax import lax
from jax.experimental import pallas as pl
from jax.experimental.pallas import tpu as pltpu
from jax.sharding import PartitionSpec as P

SUBSTEPS = 4
KEEP = 0.25
CHAIN = 12
ROUND = 3
LOADS = 5
MADE = 8


def in_vmem(x):
    return pltpu.with_memory_space_constraint(x, pltpu.VMEM)


def in_hbm(x):
    return pltpu.with_memory_space_constraint(x, pltpu.HBM)


def vmem():
    return pl.BlockSpec(memory_space=pltpu.VMEM)


def smem():
    return pl.BlockSpec(memory_space=pltpu.SMEM)


def hbm():
    return pl.BlockSpec(memory_space=pltpu.HBM)


def call(body, outs, in_specs, name, scratch=(), limit=4 << 20, aliases={}):
    return pl.pallas_call(
        body,
        out_shape=[space(shape, dtype) for space, shape, dtype in outs],
        in_specs=in_specs,
        out_specs=[smem() if space is pltpu.SMEM else vmem() for space, _, _ in outs],
        scratch_shapes=list(scratch),
        input_output_aliases=aliases,
        compiler_params=pltpu.CompilerParams(vmem_limit_bytes=limit),
        name=name,
    )


def row_update(chosen, before, after, value, one, two, coef_one, coef_two):
    width = value.shape[1]
    gathered = jnp.concatenate([chosen, before, after], axis=1)
    both = jnp.concatenate([one, two], axis=1)
    flow = jnp.dot(gathered, both, preferred_element_type=jnp.float32)
    moved = value + coef_one * flow[:, :width] + coef_two * flow[:, width:]
    return jnp.maximum(moved, KEEP * value)


def up_of(edge, opening):
    place = edge % CHAIN
    if opening:
        return 1 * (place == CHAIN - 1) + 2 * (place == CHAIN - 2) + (place % 2) * (place < CHAIN - 2)
    return 2 * (place < 5) + 1 * (place == 5) + 1 * (place == CHAIN - 1)


def down_of(edge, opening):
    place = edge % CHAIN
    if opening:
        return up_of(edge, opening)
    return 1 * (place == 5) + 1 * (place == CHAIN - 1) + 2 * (place > 5) * (place < CHAIN - 1)


def pairs_of(exchange, dom, opening):
    edges = range(dom - 1)
    return [(d, d + 1) for d in edges if up_of(d, opening) == exchange] + [
        (d + 1, d) for d in edges if down_of(d, opening) == exchange
    ]


def pick(which, parts):
    picked = parts[-1]
    for exchange in range(len(parts) - 2, -1, -1):
        picked = jnp.where(which == exchange, parts[exchange], picked)
    return picked


def halos(received, opening):
    parts = [r[...] for r in received]
    own = lax.axis_index("dom")
    return pick(up_of(own + CHAIN - 1, opening), parts), pick(down_of(own, opening), parts)


def send(outs, first, last, opening):
    to_left = down_of(lax.axis_index("dom") + CHAIN - 1, opening)
    for exchange, out in enumerate(outs):
        out[...] = jnp.where(to_left == exchange, first, last)


def chosen_block(e, left, right, blocks_ref):
    n = blocks_ref.shape[0]
    inner = blocks_ref[jnp.clip(e - 1, 0, n - 1)]
    return jnp.where(e == 0, left, jnp.where(e == n + 1, right, inner))


def edge_rows(cols, left, right, blocks_ref, first, last, one_ref, two_ref, c1, c2):
    n, rows, width = blocks_ref.shape
    return [
        row_update(
            chosen_block(cols[0, b], left, right, blocks_ref),
            left if b == 0 else blocks_ref[b - 1],
            right if b == n - 1 else blocks_ref[b + 1],
            value,
            one_ref[b].reshape(-1, width),
            two_ref[b].reshape(-1, width),
            c1,
            c2,
        )
        for b, value in ((0, first), (n - 1, last))
    ]


def edge_kernel(opening, cols, in0, in1, in2, blocks_ref, ends_ref, one_ref, two_ref, c1_ref, c2_ref, *outs):
    out0, out1, out2, ends16, ends32 = outs
    left, right = halos((in0, in1, in2), opening)
    first, last = edge_rows(
        cols, left, right, blocks_ref, ends_ref[0], ends_ref[1], one_ref, two_ref, c1_ref[...], c2_ref[...]
    )
    ends32[0], ends32[1] = first, last
    first, last = first.astype(jnp.bfloat16), last.astype(jnp.bfloat16)
    ends16[0], ends16[1] = first, last
    send((out0, out1, out2), first, last, False)


def inner_kernel(opening, cols, in0, in1, in2, blocks_ref, field_ref, ends16, one_ref, two_ref, c1_ref, c2_ref, *outs):
    out16, out32 = outs
    n, rows, width = blocks_ref.shape
    left, right = halos((in0, in1, in2), opening)
    c1, c2 = c1_ref[...], c2_ref[...]
    out16[0] = ends16[0]
    out16[n - 1] = ends16[1]
    for b in range(1, n - 1):
        new = row_update(
            chosen_block(cols[0, b], left, right, blocks_ref),
            blocks_ref[b - 1],
            blocks_ref[b + 1],
            field_ref[b],
            one_ref[b].reshape(-1, width),
            two_ref[b].reshape(-1, width),
            c1,
            c2,
        )
        out32[b] = new
        out16[b] = new.astype(jnp.bfloat16)


def last_inner_kernel(cols, blocks_ref, field_ref, one_ref, two_ref, c1_ref, c2_ref, out16):
    n, rows, width = blocks_ref.shape
    c1, c2 = c1_ref[...], c2_ref[...]
    for b in range(1, n - 1):
        new = row_update(
            blocks_ref[jnp.clip(cols[0, b] - 1, 0, n - 1)],
            blocks_ref[b - 1],
            blocks_ref[b + 1],
            field_ref[b],
            one_ref[b].reshape(-1, width),
            two_ref[b].reshape(-1, width),
            c1,
            c2,
        )
        out16[b] = new.astype(jnp.bfloat16)


def last_edge_kernel(cols, todo, in0, in1, in2, blocks_ref, field_ref, ends_ref, one_ref, two_ref, c1_ref, c2_ref, inner_ref, out16):
    n, rows, width = blocks_ref.shape
    left, right = halos((in0, in1, in2), False)
    c1, c2 = c1_ref[...], c2_ref[...]

    def again(b):
        return row_update(
            chosen_block(cols[0, b], left, right, blocks_ref),
            blocks_ref[b - 1],
            blocks_ref[b + 1],
            field_ref[b],
            one_ref[b].reshape(-1, width),
            two_ref[b].reshape(-1, width),
            c1,
            c2,
        ).astype(jnp.bfloat16)

    first, last = edge_rows(
        cols, left, right, blocks_ref, ends_ref[0], ends_ref[1], one_ref, two_ref, c1, c2
    )
    at = [todo[0, i] for i in range(ROUND)]
    new = [again(b) for b in at]
    out16[0] = first.astype(jnp.bfloat16)
    out16[n - 1] = last.astype(jnp.bfloat16)
    for b, value in zip(at, new):
        out16[b] = value

    @pl.when(todo[0, n - 1] > ROUND)
    def _():
        @pl.loop(ROUND, todo[0, n - 1])
        def _(i):
            b = todo[0, i]
            out16[b] = again(b)


def begin_kernel(action_ref, out0, out1, out2, buffers, sems):
    width = out0.shape[1]
    cells = action_ref.shape[1]
    copies = [
        pltpu.make_async_copy(action_ref.at[:, pl.ds(at, width)], buffers.at[i], sems.at[i])
        for i, at in enumerate((0, cells - width))
    ]
    for copy in copies:
        copy.start()
    for copy in copies:
        copy.wait()
    send((out0, out1, out2), buffers[0].astype(jnp.bfloat16), buffers[1].astype(jnp.bfloat16), True)


def load(sources, outs, coefs, sems):
    action_ref, coef_one_hbm, coef_two_hbm, two_hbm, cols_hbm = sources
    cols, todo, out16, out32, ends32, two, c1, c2 = outs
    n, rows, width = out16.shape
    small = [
        pltpu.make_async_copy(cols_hbm, cols, sems.at[n + 2]),
        pltpu.make_async_copy(coef_one_hbm, coefs.at[0], sems.at[n]),
        pltpu.make_async_copy(coef_two_hbm, coefs.at[1], sems.at[n + 1]),
    ]
    blocks = [
        pltpu.make_async_copy(action_ref.at[:, pl.ds(b * width, width)], out32.at[b], sems.at[b])
        for b in range(n)
    ]
    weights = pltpu.make_async_copy(two_hbm, two, sems.at[n + 3])
    for copy in small + blocks + [weights]:
        copy.start()
    for copy in small:
        copy.wait()
    for i in range(n):
        todo[0, i] = 1
    count = jnp.int32(0)
    for b in range(1, n - 1):
        e = cols[0, b]
        reads_halo = (e == 0) | (e == n + 1)

        @pl.when(reads_halo)
        def _(b=b, count=count):
            todo[0, count] = b

        count = count + reads_halo.astype(jnp.int32)
    todo[0, n - 1] = count
    c1[...] = jnp.broadcast_to(coefs[0], (width, rows)).T
    c2[...] = jnp.broadcast_to(coefs[1], (width, rows)).T
    for b in range(n):
        blocks[b].wait()
        out16[b] = out32[b].astype(jnp.bfloat16)
    ends32[0] = out32[0]
    ends32[1] = out32[n - 1]
    weights.wait()


def load_early_kernel(*refs):
    sources, outs, (coefs, sems) = refs[:LOADS], refs[LOADS + 2 : -4], refs[-2:]

    @pl.when(lax.axis_index("dom") % CHAIN == 0)
    def _():
        load(sources, outs, coefs, sems)


def load_late_kernel(*refs):
    sources, outs, (coefs, sems) = refs[:LOADS], refs[LOADS + MADE : -2], refs[-2:]

    @pl.when(lax.axis_index("dom") % CHAIN != 0)
    def _():
        load(sources, outs, coefs, sems)


def source_kernel(cells_ref, one_ref, two_ref, out_hbm, buffers, sems):
    steps, _, tile = buffers.shape
    cells = cells_ref[...].T
    copies = []
    for i in range(steps):
        at = slice(i * tile, (i + 1) * tile)
        own = cells[:, at].astype(jnp.float32)
        quads = jnp.concatenate([one_ref[:, at], two_ref[:, at]], axis=1)
        both = jnp.dot(cells, quads, preferred_element_type=jnp.float32)
        first, second = both[:, :tile], both[:, tile:]
        buffers[i] = own + 0.5 * (first * own - second * own * own)
        copies.append(pltpu.make_async_copy(buffers.at[i], out_hbm.at[0, :, pl.ds(i * tile, tile)], sems.at[i]))
        copies[-1].start()
    for copy in copies:
        copy.wait()


def source_terms(exchanged, quad_one, quad_two):
    comps, cells = exchanged.shape
    tile = 128
    steps = comps // tile
    return pl.pallas_call(
        source_kernel,
        out_shape=jax.ShapeDtypeStruct((1, cells, comps), jnp.float32),
        in_specs=[vmem()] * 3,
        out_specs=hbm(),
        scratch_shapes=[
            pltpu.VMEM((steps, cells, tile), jnp.float32),
            pltpu.SemaphoreType.DMA((steps,)),
        ],
        compiler_params=pltpu.CompilerParams(vmem_limit_bytes=8 << 20),
        name="source_terms",
    )(in_vmem(exchanged), in_vmem(quad_one), in_vmem(quad_two))


def per_device(
    action, coef_one, coef_two, transport_one, transport_two, block_cols, quad_one, quad_two
):
    rows, cells_dev = action.shape
    n, nnz, width, _ = transport_one.shape
    dom = lax.axis_size("dom")
    bf16, f32 = jnp.bfloat16, jnp.float32
    block, blocks, ends, weights = (rows, width), (n, rows, width), (2, rows, width), (n, nnz, width, width)
    vm = lambda shape, dtype: (pltpu.VMEM, shape, dtype)
    sm = lambda shape: (pltpu.SMEM, shape, jnp.int32)
    exchange = lambda parts, opening: [
        in_vmem(lax.ppermute(x, "dom", pairs_of(i, dom, opening))) for i, x in enumerate(parts)
    ]

    out_part, boundary_part, back_part = call(
        begin_kernel,
        [vm(block, bf16)] * 3,
        [hbm()],
        "begin",
        [pltpu.VMEM((2, rows, width), f32), pltpu.SemaphoreType.DMA((2,))],
    )(in_hbm(action))
    sources = [
        in_hbm(x)
        for x in (
            action,
            coef_one.reshape(1, rows),
            coef_two.reshape(1, rows),
            transport_two,
            block_cols.T,
        )
    ]
    made = [sm((nnz, n)), sm((1, n)), vm(blocks, bf16), vm(blocks, f32), vm(ends, f32)]
    made += [vm(weights, bf16)] + [vm(block, f32)] * 2
    room = [pltpu.VMEM((2, 1, rows), f32), pltpu.SemaphoreType.DMA((n + 4,))]
    *loaded, boundary_part, back_part = call(
        load_early_kernel,
        made + [vm(block, bf16)] * 2,
        [hbm()] * LOADS + [vmem()] * 2,
        "load_early",
        room,
        aliases={LOADS: MADE, LOADS + 1: MADE + 1},
    )(*sources, boundary_part, back_part)
    received = exchange((out_part, boundary_part, back_part), True)
    cols, todo, value16, value32, ends32, two, c1, c2 = call(
        load_late_kernel,
        made,
        [hbm()] * LOADS + [smem()] * 2 + [vmem()] * (MADE - 2),
        "load_late",
        room,
        aliases={LOADS + i: i for i in range(MADE)},
    )(*sources, *loaded)
    one = in_vmem(transport_one)
    for substep in range(SUBSTEPS - 1):
        *parts, ends16, ends32 = call(
            functools.partial(edge_kernel, substep == 0),
            [vm(block, bf16)] * 3 + [vm(ends, bf16), vm(ends, f32)],
            [smem()] + [vmem()] * 9,
            "edges",
        )(cols, *received, value16, ends32, one, two, c1, c2)
        new_received = exchange(parts, False)
        value16, value32 = call(
            functools.partial(inner_kernel, substep == 0), [vm(blocks, bf16), vm(blocks, f32)], [smem()] + [vmem()] * 10, "inner"
        )(cols, *received, value16, value32, ends16, one, two, c1, c2)
        received = new_received
    (final,) = call(last_inner_kernel, [vm(blocks, bf16)], [smem()] + [vmem()] * 6, "last_inner")(
        cols, value16, value32, one, two, c1, c2
    )
    (final,) = call(
        last_edge_kernel, [vm(blocks, bf16)], [smem()] * 2 + [vmem()] * 11, "last_edge", aliases={12: 0}
    )(cols, todo, *received, value16, value32, ends32, one, two, c1, c2, final)
    exchanged = lax.all_to_all(final, "comp", split_axis=0, concat_axis=0, tiled=True)
    return source_terms(exchanged.reshape(n * rows, width), quad_one, quad_two)


def solution(mesh):
    in_specs = (
        P("comp", "dom"),
        P("comp"),
        P("comp"),
        P("dom", None, None, None),
        P("dom", None, None, None),
        P("dom", None),
        P(),
        P(),
    )
    out_specs = P("dom", "comp", None)
    return jax.shard_map(
        per_device, mesh=mesh, in_specs=in_specs, out_specs=out_specs, check_vma=False
    )
```

```python
import functools

import jax
import jax.numpy as jnp
from jax import lax
from jax.experimental import pallas as pl
from jax.experimental.pallas import tpu as pltpu
from jax.sharding import PartitionSpec as P

SUBSTEPS = 4
KEEP = 0.25
CHAIN = 12
ROUND = 3


def in_vmem(x):
    return pltpu.with_memory_space_constraint(x, pltpu.VMEM)


def in_hbm(x):
    return pltpu.with_memory_space_constraint(x, pltpu.HBM)


def vmem():
    return pl.BlockSpec(memory_space=pltpu.VMEM)


def smem():
    return pl.BlockSpec(memory_space=pltpu.SMEM)


def hbm():
    return pl.BlockSpec(memory_space=pltpu.HBM)


def call(body, outs, in_specs, name, scratch=(), limit=4 << 20, aliases={}):
    return pl.pallas_call(
        body,
        out_shape=[space(shape, dtype) for space, shape, dtype in outs],
        in_specs=in_specs,
        out_specs=[smem() if space is pltpu.SMEM else vmem() for space, _, _ in outs],
        scratch_shapes=list(scratch),
        input_output_aliases=aliases,
        compiler_params=pltpu.CompilerParams(vmem_limit_bytes=limit),
        name=name,
    )


def row_update(chosen, before, after, value, one, two, coef_one, coef_two):
    width = value.shape[1]
    gathered = jnp.concatenate([chosen, before, after], axis=1)
    both = jnp.concatenate([one, two], axis=1)
    flow = jnp.dot(gathered, both, preferred_element_type=jnp.float32)
    moved = value + coef_one * flow[:, :width] + coef_two * flow[:, width:]
    return jnp.maximum(moved, KEEP * value)


def up_of(edge, opening):
    place = edge % CHAIN
    if opening:
        return 1 * (place == CHAIN - 1) + 1 * (place == CHAIN - 3) + 2 * (place % 2) * (place < CHAIN - 3)
    return 2 * (place < 5) + 1 * (place == 5) + 1 * (place == CHAIN - 1)


def down_of(edge, opening):
    place = edge % CHAIN
    if opening:
        return 1 * (place == CHAIN - 1) + 2 * (place == CHAIN - 2) + 2 * (place % 2) * (place < CHAIN - 2)
    return 1 * (place == 5) + 1 * (place == CHAIN - 1) + 2 * (place > 5) * (place < CHAIN - 1)


def pairs_of(exchange, dom, opening):
    edges = range(dom - 1)
    return [(d, d + 1) for d in edges if up_of(d, opening) == exchange] + [
        (d + 1, d) for d in edges if down_of(d, opening) == exchange
    ]


def pick(which, parts):
    picked = parts[-1]
    for exchange in range(len(parts) - 2, -1, -1):
        picked = jnp.where(which == exchange, parts[exchange], picked)
    return picked


def halos(received, opening):
    parts = [r[...] for r in received]
    own = lax.axis_index("dom")
    return pick(up_of(own + CHAIN - 1, opening), parts), pick(down_of(own, opening), parts)


def send(outs, first, last, opening):
    to_left = down_of(lax.axis_index("dom") + CHAIN - 1, opening)
    for exchange, out in enumerate(outs):
        out[...] = jnp.where(to_left == exchange, first, last)


def chosen_block(e, left, right, blocks_ref):
    n = blocks_ref.shape[0]
    inner = blocks_ref[jnp.clip(e - 1, 0, n - 1)]
    return jnp.where(e == 0, left, jnp.where(e == n + 1, right, inner))


def edge_rows(cols, left, right, blocks_ref, first, last, one_ref, two_ref, c1, c2):
    n, rows, width = blocks_ref.shape
    return [
        row_update(
            chosen_block(cols[0, b], left, right, blocks_ref),
            left if b == 0 else blocks_ref[b - 1],
            right if b == n - 1 else blocks_ref[b + 1],
            value,
            one_ref[b].reshape(-1, width),
            two_ref[b].reshape(-1, width),
            c1,
            c2,
        )
        for b, value in ((0, first), (n - 1, last))
    ]


def edge_kernel(opening, cols, in0, in1, in2, blocks_ref, ends_ref, one_ref, two_ref, c1_ref, c2_ref, *outs):
    out0, out1, out2, ends16, ends32 = outs
    left, right = halos((in0, in1, in2), opening)
    first, last = edge_rows(
        cols, left, right, blocks_ref, ends_ref[0], ends_ref[1], one_ref, two_ref, c1_ref[...], c2_ref[...]
    )
    ends32[0], ends32[1] = first, last
    first, last = first.astype(jnp.bfloat16), last.astype(jnp.bfloat16)
    ends16[0], ends16[1] = first, last
    send((out0, out1, out2), first, last, False)


def inner_kernel(opening, cols, in0, in1, in2, blocks_ref, field_ref, ends16, one_ref, two_ref, c1_ref, c2_ref, *outs):
    out16, out32 = outs
    n, rows, width = blocks_ref.shape
    left, right = halos((in0, in1, in2), opening)
    c1, c2 = c1_ref[...], c2_ref[...]
    out16[0] = ends16[0]
    out16[n - 1] = ends16[1]
    for b in range(1, n - 1):
        new = row_update(
            chosen_block(cols[0, b], left, right, blocks_ref),
            blocks_ref[b - 1],
            blocks_ref[b + 1],
            field_ref[b],
            one_ref[b].reshape(-1, width),
            two_ref[b].reshape(-1, width),
            c1,
            c2,
        )
        out32[b] = new
        out16[b] = new.astype(jnp.bfloat16)


def last_inner_kernel(cols, blocks_ref, field_ref, one_ref, two_ref, c1_ref, c2_ref, out16):
    n, rows, width = blocks_ref.shape
    c1, c2 = c1_ref[...], c2_ref[...]
    for b in range(1, n - 1):
        new = row_update(
            blocks_ref[jnp.clip(cols[0, b] - 1, 0, n - 1)],
            blocks_ref[b - 1],
            blocks_ref[b + 1],
            field_ref[b],
            one_ref[b].reshape(-1, width),
            two_ref[b].reshape(-1, width),
            c1,
            c2,
        )
        out16[b] = new.astype(jnp.bfloat16)


def last_edge_kernel(cols, todo, in0, in1, in2, blocks_ref, field_ref, ends_ref, one_ref, two_ref, c1_ref, c2_ref, inner_ref, out16):
    n, rows, width = blocks_ref.shape
    left, right = halos((in0, in1, in2), False)
    c1, c2 = c1_ref[...], c2_ref[...]

    def again(b):
        return row_update(
            chosen_block(cols[0, b], left, right, blocks_ref),
            blocks_ref[b - 1],
            blocks_ref[b + 1],
            field_ref[b],
            one_ref[b].reshape(-1, width),
            two_ref[b].reshape(-1, width),
            c1,
            c2,
        ).astype(jnp.bfloat16)

    first, last = edge_rows(
        cols, left, right, blocks_ref, ends_ref[0], ends_ref[1], one_ref, two_ref, c1, c2
    )
    at = [todo[0, i] for i in range(ROUND)]
    new = [again(b) for b in at]
    out16[0] = first.astype(jnp.bfloat16)
    out16[n - 1] = last.astype(jnp.bfloat16)
    for b, value in zip(at, new):
        out16[b] = value

    @pl.when(todo[0, n - 1] > ROUND)
    def _():
        @pl.loop(ROUND, todo[0, n - 1])
        def _(i):
            b = todo[0, i]
            out16[b] = again(b)


def begin_kernel(action_ref, out0, out1, out2, buffers, sems):
    width = out0.shape[1]
    cells = action_ref.shape[1]
    copies = [
        pltpu.make_async_copy(action_ref.at[:, pl.ds(at, width)], buffers.at[i], sems.at[i])
        for i, at in enumerate((0, cells - width))
    ]
    for copy in copies:
        copy.start()
    for copy in copies:
        copy.wait()
    send((out0, out1, out2), buffers[0].astype(jnp.bfloat16), buffers[1].astype(jnp.bfloat16), True)


def load_kernel(action_ref, coef_one_hbm, coef_two_hbm, two_hbm, cols_hbm, *refs):
    cols, todo, out16, out32, ends32, two, c1, c2, coefs, sems = refs
    n, rows, width = out16.shape
    small = [
        pltpu.make_async_copy(cols_hbm, cols, sems.at[n + 2]),
        pltpu.make_async_copy(coef_one_hbm, coefs.at[0], sems.at[n]),
        pltpu.make_async_copy(coef_two_hbm, coefs.at[1], sems.at[n + 1]),
    ]
    blocks = [
        pltpu.make_async_copy(action_ref.at[:, pl.ds(b * width, width)], out32.at[b], sems.at[b])
        for b in range(n)
    ]
    weights = pltpu.make_async_copy(two_hbm, two, sems.at[n + 3])
    for copy in small + blocks + [weights]:
        copy.start()
    for copy in small:
        copy.wait()
    for i in range(n):
        todo[0, i] = 1
    count = jnp.int32(0)
    for b in range(1, n - 1):
        e = cols[0, b]
        reads_halo = (e == 0) | (e == n + 1)

        @pl.when(reads_halo)
        def _(b=b, count=count):
            todo[0, count] = b

        count = count + reads_halo.astype(jnp.int32)
    todo[0, n - 1] = count
    c1[...] = jnp.broadcast_to(coefs[0], (width, rows)).T
    c2[...] = jnp.broadcast_to(coefs[1], (width, rows)).T
    for b in range(n):
        blocks[b].wait()
        out16[b] = out32[b].astype(jnp.bfloat16)
    ends32[0] = out32[0]
    ends32[1] = out32[n - 1]
    weights.wait()


def source_kernel(cells_ref, one_ref, two_ref, out_hbm, buffers, sems):
    steps, _, tile = buffers.shape
    cells = cells_ref[...].T
    copies = []
    for i in range(steps):
        at = slice(i * tile, (i + 1) * tile)
        own = cells[:, at].astype(jnp.float32)
        quads = jnp.concatenate([one_ref[:, at], two_ref[:, at]], axis=1)
        both = jnp.dot(cells, quads, preferred_element_type=jnp.float32)
        first, second = both[:, :tile], both[:, tile:]
        buffers[i] = own + 0.5 * (first * own - second * own * own)
        copies.append(pltpu.make_async_copy(buffers.at[i], out_hbm.at[0, :, pl.ds(i * tile, tile)], sems.at[i]))
        copies[-1].start()
    for copy in copies:
        copy.wait()


def source_terms(exchanged, quad_one, quad_two):
    comps, cells = exchanged.shape
    tile = 128
    steps = comps // tile
    return pl.pallas_call(
        source_kernel,
        out_shape=jax.ShapeDtypeStruct((1, cells, comps), jnp.float32),
        in_specs=[vmem()] * 3,
        out_specs=hbm(),
        scratch_shapes=[
            pltpu.VMEM((steps, cells, tile), jnp.float32),
            pltpu.SemaphoreType.DMA((steps,)),
        ],
        compiler_params=pltpu.CompilerParams(vmem_limit_bytes=8 << 20),
        name="source_terms",
    )(in_vmem(exchanged), in_vmem(quad_one), in_vmem(quad_two))


def per_device(
    action, coef_one, coef_two, transport_one, transport_two, block_cols, quad_one, quad_two
):
    rows, cells_dev = action.shape
    n, nnz, width, _ = transport_one.shape
    dom = lax.axis_size("dom")
    bf16, f32 = jnp.bfloat16, jnp.float32
    block, blocks, ends, weights = (rows, width), (n, rows, width), (2, rows, width), (n, nnz, width, width)
    vm = lambda shape, dtype: (pltpu.VMEM, shape, dtype)
    sm = lambda shape: (pltpu.SMEM, shape, jnp.int32)
    exchange = lambda parts, opening: [
        in_vmem(lax.ppermute(x, "dom", pairs_of(i, dom, opening))) for i, x in enumerate(parts)
    ]

    received = exchange(
        call(
            begin_kernel,
            [vm(block, bf16)] * 3,
            [hbm()],
            "begin",
            [pltpu.VMEM((2, rows, width), f32), pltpu.SemaphoreType.DMA((2,))],
        )(in_hbm(action)),
        True,
    )
    cols, todo, value16, value32, ends32, two, c1, c2 = call(
        load_kernel,
        [sm((nnz, n)), sm((1, n)), vm(blocks, bf16), vm(blocks, f32), vm(ends, f32)]
        + [vm(weights, bf16), vm(block, f32), vm(block, f32)],
        [hbm()] * 5,
        "load",
        [pltpu.VMEM((2, 1, rows), f32), pltpu.SemaphoreType.DMA((n + 4,))],
    )(
        in_hbm(action),
        in_hbm(coef_one.reshape(1, rows)),
        in_hbm(coef_two.reshape(1, rows)),
        in_hbm(transport_two),
        in_hbm(block_cols.T),
    )
    one = in_vmem(transport_one)
    for substep in range(SUBSTEPS - 1):
        *parts, ends16, ends32 = call(
            functools.partial(edge_kernel, substep == 0),
            [vm(block, bf16)] * 3 + [vm(ends, bf16), vm(ends, f32)],
            [smem()] + [vmem()] * 9,
            "edges",
        )(cols, *received, value16, ends32, one, two, c1, c2)
        new_received = exchange(parts, False)
        value16, value32 = call(
            functools.partial(inner_kernel, substep == 0), [vm(blocks, bf16), vm(blocks, f32)], [smem()] + [vmem()] * 10, "inner"
        )(cols, *received, value16, value32, ends16, one, two, c1, c2)
        received = new_received
    (final,) = call(last_inner_kernel, [vm(blocks, bf16)], [smem()] + [vmem()] * 6, "last_inner")(
        cols, value16, value32, one, two, c1, c2
    )
    (final,) = call(
        last_edge_kernel, [vm(blocks, bf16)], [smem()] * 2 + [vmem()] * 11, "last_edge", aliases={12: 0}
    )(cols, todo, *received, value16, value32, ends32, one, two, c1, c2, final)
    exchanged = lax.all_to_all(final, "comp", split_axis=0, concat_axis=0, tiled=True)
    return source_terms(exchanged.reshape(n * rows, width), quad_one, quad_two)


def solution(mesh):
    in_specs = (
        P("comp", "dom"),
        P("comp"),
        P("comp"),
        P("dom", None, None, None),
        P("dom", None, None, None),
        P("dom", None),
        P(),
        P(),
    )
    out_specs = P("dom", "comp", None)
    return jax.shard_map(
        per_device, mesh=mesh, in_specs=in_specs, out_specs=out_specs, check_vma=False
    )
```

```python
import functools

import jax
import jax.numpy as jnp
from jax import lax
from jax.experimental import pallas as pl
from jax.experimental.pallas import tpu as pltpu
from jax.sharding import PartitionSpec as P

SUBSTEPS = 4
KEEP = 0.25
CHAIN = 12
TURN = 7
ROUND = 3


def in_vmem(x):
    return pltpu.with_memory_space_constraint(x, pltpu.VMEM)


def in_hbm(x):
    return pltpu.with_memory_space_constraint(x, pltpu.HBM)


def vmem():
    return pl.BlockSpec(memory_space=pltpu.VMEM)


def smem():
    return pl.BlockSpec(memory_space=pltpu.SMEM)


def hbm():
    return pl.BlockSpec(memory_space=pltpu.HBM)


def call(body, outs, in_specs, name, scratch=(), limit=4 << 20, aliases={}):
    return pl.pallas_call(
        body,
        out_shape=[space(shape, dtype) for space, shape, dtype in outs],
        in_specs=in_specs,
        out_specs=[smem() if space is pltpu.SMEM else vmem() for space, _, _ in outs],
        scratch_shapes=list(scratch),
        input_output_aliases=aliases,
        compiler_params=pltpu.CompilerParams(vmem_limit_bytes=limit),
        name=name,
    )


def row_update(chosen, before, after, value, one, two, coef_one, coef_two):
    width = value.shape[1]
    gathered = jnp.concatenate([chosen, before, after], axis=1)
    both = jnp.concatenate([one, two], axis=1)
    flow = jnp.dot(gathered, both, preferred_element_type=jnp.float32)
    moved = value + coef_one * flow[:, :width] + coef_two * flow[:, width:]
    return jnp.maximum(moved, KEEP * value)


def up_of(edge, opening):
    place = edge % CHAIN
    if opening:
        return 1 * (place == CHAIN - 1) + 1 * (place == CHAIN - 3) + 2 * (place % 2) * (place < CHAIN - 3)
    return 2 * (place < TURN) + 1 * (place == TURN) + 1 * (place == CHAIN - 1)


def down_of(edge, opening):
    place = edge % CHAIN
    if opening:
        return 1 * (place == CHAIN - 1) + 2 * (place == CHAIN - 2) + 2 * (place % 2) * (place < CHAIN - 2)
    return 1 * (place == TURN) + 1 * (place == CHAIN - 1) + 2 * (place > TURN) * (place < CHAIN - 1)


def pairs_of(exchange, dom, opening):
    edges = range(dom - 1)
    return [(d, d + 1) for d in edges if up_of(d, opening) == exchange] + [
        (d + 1, d) for d in edges if down_of(d, opening) == exchange
    ]


def pick(which, parts):
    picked = parts[-1]
    for exchange in range(len(parts) - 2, -1, -1):
        picked = jnp.where(which == exchange, parts[exchange], picked)
    return picked


def halos(received, opening):
    parts = [r[...] for r in received]
    own = lax.axis_index("dom")
    return pick(up_of(own + CHAIN - 1, opening), parts), pick(down_of(own, opening), parts)


def send(outs, first, last, opening):
    to_left = down_of(lax.axis_index("dom") + CHAIN - 1, opening)
    for exchange, out in enumerate(outs):
        out[...] = jnp.where(to_left == exchange, first, last)


def chosen_block(e, left, right, blocks_ref):
    n = blocks_ref.shape[0]
    inner = blocks_ref[jnp.clip(e - 1, 0, n - 1)]
    return jnp.where(e == 0, left, jnp.where(e == n + 1, right, inner))


def edge_rows(cols, left, right, blocks_ref, first, last, one_ref, two_ref, c1, c2):
    n, rows, width = blocks_ref.shape
    return [
        row_update(
            chosen_block(cols[0, b], left, right, blocks_ref),
            left if b == 0 else blocks_ref[b - 1],
            right if b == n - 1 else blocks_ref[b + 1],
            value,
            one_ref[b].reshape(-1, width),
            two_ref[b].reshape(-1, width),
            c1,
            c2,
        )
        for b, value in ((0, first), (n - 1, last))
    ]


def edge_kernel(opening, cols, in0, in1, in2, blocks_ref, ends_ref, one_ref, two_ref, c1_ref, c2_ref, *outs):
    out0, out1, out2, ends16, ends32 = outs
    left, right = halos((in0, in1, in2), opening)
    first, last = edge_rows(
        cols, left, right, blocks_ref, ends_ref[0], ends_ref[1], one_ref, two_ref, c1_ref[...], c2_ref[...]
    )
    ends32[0], ends32[1] = first, last
    first, last = first.astype(jnp.bfloat16), last.astype(jnp.bfloat16)
    ends16[0], ends16[1] = first, last
    send((out0, out1, out2), first, last, False)


def inner_kernel(opening, cols, in0, in1, in2, blocks_ref, field_ref, ends16, one_ref, two_ref, c1_ref, c2_ref, *outs):
    out16, out32 = outs
    n, rows, width = blocks_ref.shape
    left, right = halos((in0, in1, in2), opening)
    c1, c2 = c1_ref[...], c2_ref[...]
    out16[0] = ends16[0]
    out16[n - 1] = ends16[1]
    for b in range(1, n - 1):
        new = row_update(
            chosen_block(cols[0, b], left, right, blocks_ref),
            blocks_ref[b - 1],
            blocks_ref[b + 1],
            field_ref[b],
            one_ref[b].reshape(-1, width),
            two_ref[b].reshape(-1, width),
            c1,
            c2,
        )
        out32[b] = new
        out16[b] = new.astype(jnp.bfloat16)


def last_inner_kernel(cols, blocks_ref, field_ref, one_ref, two_ref, c1_ref, c2_ref, out16):
    n, rows, width = blocks_ref.shape
    c1, c2 = c1_ref[...], c2_ref[...]
    for b in range(1, n - 1):
        new = row_update(
            blocks_ref[jnp.clip(cols[0, b] - 1, 0, n - 1)],
            blocks_ref[b - 1],
            blocks_ref[b + 1],
            field_ref[b],
            one_ref[b].reshape(-1, width),
            two_ref[b].reshape(-1, width),
            c1,
            c2,
        )
        out16[b] = new.astype(jnp.bfloat16)


def last_edge_kernel(cols, todo, in0, in1, in2, blocks_ref, field_ref, ends_ref, one_ref, two_ref, c1_ref, c2_ref, inner_ref, out16):
    n, rows, width = blocks_ref.shape
    left, right = halos((in0, in1, in2), False)
    c1, c2 = c1_ref[...], c2_ref[...]

    def again(b):
        return row_update(
            chosen_block(cols[0, b], left, right, blocks_ref),
            blocks_ref[b - 1],
            blocks_ref[b + 1],
            field_ref[b],
            one_ref[b].reshape(-1, width),
            two_ref[b].reshape(-1, width),
            c1,
            c2,
        ).astype(jnp.bfloat16)

    first, last = edge_rows(
        cols, left, right, blocks_ref, ends_ref[0], ends_ref[1], one_ref, two_ref, c1, c2
    )
    at = [todo[0, i] for i in range(ROUND)]
    new = [again(b) for b in at]
    out16[0] = first.astype(jnp.bfloat16)
    out16[n - 1] = last.astype(jnp.bfloat16)
    for b, value in zip(at, new):
        out16[b] = value

    @pl.when(todo[0, n - 1] > ROUND)
    def _():
        @pl.loop(ROUND, todo[0, n - 1])
        def _(i):
            b = todo[0, i]
            out16[b] = again(b)


def begin_kernel(action_ref, out0, out1, out2, buffers, sems):
    width = out0.shape[1]
    cells = action_ref.shape[1]
    copies = [
        pltpu.make_async_copy(action_ref.at[:, pl.ds(at, width)], buffers.at[i], sems.at[i])
        for i, at in enumerate((0, cells - width))
    ]
    for copy in copies:
        copy.start()
    for copy in copies:
        copy.wait()
    send((out0, out1, out2), buffers[0].astype(jnp.bfloat16), buffers[1].astype(jnp.bfloat16), True)


def load_kernel(action_ref, coef_one_hbm, coef_two_hbm, two_hbm, cols_hbm, *refs):
    cols, todo, out16, out32, ends32, two, c1, c2, coefs, sems = refs
    n, rows, width = out16.shape
    small = [
        pltpu.make_async_copy(cols_hbm, cols, sems.at[n + 2]),
        pltpu.make_async_copy(coef_one_hbm, coefs.at[0], sems.at[n]),
        pltpu.make_async_copy(coef_two_hbm, coefs.at[1], sems.at[n + 1]),
    ]
    blocks = [
        pltpu.make_async_copy(action_ref.at[:, pl.ds(b * width, width)], out32.at[b], sems.at[b])
        for b in range(n)
    ]
    weights = pltpu.make_async_copy(two_hbm, two, sems.at[n + 3])
    for copy in small + blocks + [weights]:
        copy.start()
    for copy in small:
        copy.wait()
    for i in range(n):
        todo[0, i] = 1
    count = jnp.int32(0)
    for b in range(1, n - 1):
        e = cols[0, b]
        reads_halo = (e == 0) | (e == n + 1)

        @pl.when(reads_halo)
        def _(b=b, count=count):
            todo[0, count] = b

        count = count + reads_halo.astype(jnp.int32)
    todo[0, n - 1] = count
    c1[...] = jnp.broadcast_to(coefs[0], (width, rows)).T
    c2[...] = jnp.broadcast_to(coefs[1], (width, rows)).T
    for b in range(n):
        blocks[b].wait()
        out16[b] = out32[b].astype(jnp.bfloat16)
    ends32[0] = out32[0]
    ends32[1] = out32[n - 1]
    weights.wait()


def source_kernel(cells_ref, one_ref, two_ref, out_hbm, buffers, sems):
    steps, _, tile = buffers.shape
    cells = cells_ref[...].T
    copies = []
    for i in range(steps):
        at = slice(i * tile, (i + 1) * tile)
        own = cells[:, at].astype(jnp.float32)
        quads = jnp.concatenate([one_ref[:, at], two_ref[:, at]], axis=1)
        both = jnp.dot(cells, quads, preferred_element_type=jnp.float32)
        first, second = both[:, :tile], both[:, tile:]
        buffers[i] = own + 0.5 * (first * own - second * own * own)
        copies.append(pltpu.make_async_copy(buffers.at[i], out_hbm.at[0, :, pl.ds(i * tile, tile)], sems.at[i]))
        copies[-1].start()
    for copy in copies:
        copy.wait()


def source_terms(exchanged, quad_one, quad_two):
    comps, cells = exchanged.shape
    tile = 128
    steps = comps // tile
    return pl.pallas_call(
        source_kernel,
        out_shape=jax.ShapeDtypeStruct((1, cells, comps), jnp.float32),
        in_specs=[vmem()] * 3,
        out_specs=hbm(),
        scratch_shapes=[
            pltpu.VMEM((steps, cells, tile), jnp.float32),
            pltpu.SemaphoreType.DMA((steps,)),
        ],
        compiler_params=pltpu.CompilerParams(vmem_limit_bytes=8 << 20),
        name="source_terms",
    )(in_vmem(exchanged), in_vmem(quad_one), in_vmem(quad_two))


def per_device(
    action, coef_one, coef_two, transport_one, transport_two, block_cols, quad_one, quad_two
):
    rows, cells_dev = action.shape
    n, nnz, width, _ = transport_one.shape
    dom = lax.axis_size("dom")
    bf16, f32 = jnp.bfloat16, jnp.float32
    block, blocks, ends, weights = (rows, width), (n, rows, width), (2, rows, width), (n, nnz, width, width)
    vm = lambda shape, dtype: (pltpu.VMEM, shape, dtype)
    sm = lambda shape: (pltpu.SMEM, shape, jnp.int32)
    exchange = lambda parts, opening: [
        in_vmem(lax.ppermute(x, "dom", pairs_of(i, dom, opening))) for i, x in enumerate(parts)
    ]

    received = exchange(
        call(
            begin_kernel,
            [vm(block, bf16)] * 3,
            [hbm()],
            "begin",
            [pltpu.VMEM((2, rows, width), f32), pltpu.SemaphoreType.DMA((2,))],
        )(in_hbm(action)),
        True,
    )
    cols, todo, value16, value32, ends32, two, c1, c2 = call(
        load_kernel,
        [sm((nnz, n)), sm((1, n)), vm(blocks, bf16), vm(blocks, f32), vm(ends, f32)]
        + [vm(weights, bf16), vm(block, f32), vm(block, f32)],
        [hbm()] * 5,
        "load",
        [pltpu.VMEM((2, 1, rows), f32), pltpu.SemaphoreType.DMA((n + 4,))],
    )(
        in_hbm(action),
        in_hbm(coef_one.reshape(1, rows)),
        in_hbm(coef_two.reshape(1, rows)),
        in_hbm(transport_two),
        in_hbm(block_cols.T),
    )
    one = in_vmem(transport_one)
    for substep in range(SUBSTEPS - 1):
        *parts, ends16, ends32 = call(
            functools.partial(edge_kernel, substep == 0),
            [vm(block, bf16)] * 3 + [vm(ends, bf16), vm(ends, f32)],
            [smem()] + [vmem()] * 9,
            "edges",
        )(cols, *received, value16, ends32, one, two, c1, c2)
        new_received = exchange(parts, False)
        value16, value32 = call(
            functools.partial(inner_kernel, substep == 0), [vm(blocks, bf16), vm(blocks, f32)], [smem()] + [vmem()] * 10, "inner"
        )(cols, *received, value16, value32, ends16, one, two, c1, c2)
        received = new_received
    (final,) = call(last_inner_kernel, [vm(blocks, bf16)], [smem()] + [vmem()] * 6, "last_inner")(
        cols, value16, value32, one, two, c1, c2
    )
    (final,) = call(
        last_edge_kernel, [vm(blocks, bf16)], [smem()] * 2 + [vmem()] * 11, "last_edge", aliases={12: 0}
    )(cols, todo, *received, value16, value32, ends32, one, two, c1, c2, final)
    exchanged = lax.all_to_all(final, "comp", split_axis=0, concat_axis=0, tiled=True)
    return source_terms(exchanged.reshape(n * rows, width), quad_one, quad_two)


def solution(mesh):
    in_specs = (
        P("comp", "dom"),
        P("comp"),
        P("comp"),
        P("dom", None, None, None),
        P("dom", None, None, None),
        P("dom", None),
        P(),
        P(),
    )
    out_specs = P("dom", "comp", None)
    return jax.shard_map(
        per_device, mesh=mesh, in_specs=in_specs, out_specs=out_specs, check_vma=False
    )
```
